1024 devices in a mesh: dp: 16 (over z_lo, core), px: 4 (over x), py: 16 (over y, z_hi).
Axes of the slice: x: 4, y: 4, z: 32 (z_hi: 4, z_lo: 8; z = z_hi * 8 + z_lo), core: 2. Of those that a mesh axis runs over, the one named last changes fastest.
Arguments:
- activations: bfloat16 [16, 64, 16, 64, 128], P('dp', None, 'px', 'py'), may hold values from -6 to 6
- grad_out: bfloat16 [16, 64, 16, 64, 128], P('dp', None, 'px', 'py'), may hold values from -6 to 6
- kernel: bfloat16 [64, 1728], replicated, may hold values from -0.15625 to 0.15625
Outputs:
- grad_input: bfloat16 [16, 64, 16, 64, 128], P('dp', None, 'px', 'py')
- grad_kernel: float32 [64, 1728], P('dp')
The draws below stay inside these ranges and needn't reach their ends.
All inputs are finite; a program needn't handle non-finite values.
Results may differ from the reference program's by a relative error of at most 0.001.
Values may be sent and summed in bfloat16 or wider, within the bound.
No kernel may reach another device: no remote copies, remote signals or barrier semaphores. Data moves between devices by JAX's collectives and lax.ppermute only.
A program may use at most 32 MiB of HBM per device.

```python
import math
import jax
import jax.numpy as jnp
from jax import lax

C_IN = 64
C_OUT = 64
NX = 16
NY = 64
NZ = 128
SAMPLES = 16


def strengthened(array, stream_key, source, target, parts, factor):
    owner, partner = [(jnp.arange(array.shape[position]) // (array.shape[position] // parts)).reshape([-1 if axis == position else 1 for axis in range(array.ndim)]) for position in (source, target)]
    chosen = jax.random.permutation(stream_key, parts)[partner]
    strong = (owner == chosen) | (owner == (partner + parts // 2) % parts)
    return jnp.where(strong, factor * array, array)


def level_of(key, dims, cuts, smallest, high):
    gain, own = 1.0, jax.random.fold_in(key, 6)
    for dim, shards_of in cuts:
        heights = jnp.exp(jax.random.uniform(jax.random.fold_in(own, dim), (shards_of,), jnp.float32, smallest / len(cuts), high / len(cuts)))
        gain = gain * jnp.repeat(heights, dims[dim] // shards_of).reshape([-1 if axis == dim else 1 for axis in range(len(dims))])
    return gain


def gaussian(rng, extent, width, most, cuts=(), kind=jnp.bfloat16):
    gain = level_of(rng, extent, cuts, -0.22, 0.18) if cuts else 1.0
    drawn = jax.random.normal(rng, extent, jnp.float32) * width * gain
    return jnp.minimum(jnp.maximum(drawn, -most), most).astype(kind)


def bell_draw_with(stream_key, extent, deviation, most, cuts, heavy, kind=jnp.bfloat16):
    values = deviation * jax.random.normal(stream_key, extent, jnp.float32)
    if cuts:
        values = values * level_of(stream_key, extent, cuts, -0.22, 0.18)
    return jnp.clip(strengthened(values, jax.random.fold_in(stream_key, 3), *heavy), -most, most).astype(kind)


def setup_inputs(seed: int = 0) -> dict:
    key_list = jax.random.split(jax.random.key(seed), 4)
    return {
        "activations": gaussian(key_list[0], (SAMPLES, C_IN, NX, NY, NZ), 1.0, 6.0, ((0, 16), (2, 4), (3, 16))),
        "grad_out": bell_draw_with(key_list[1], (SAMPLES, C_OUT, NX, NY, NZ), 1.0, 6.0, ((0, 16), (2, 4), (3, 16)), (0, 1, 16, 2.0)),
        "kernel": gaussian(key_list[2], (C_OUT, 27 * C_IN), (27 * C_OUT) ** -0.5, 0.15625),
    }


def one_sample(pair, kernel):
    activ, grads = pair
    in_channels = activ.shape[0]
    out_channels = grads.shape[0]
    cells = NX * NY * NZ
    padded = jnp.pad(grads, ((0, 0), (1, 1), (1, 1), (1, 1)))
    flat_activ = activ.reshape(in_channels, cells)
    total = jnp.zeros((in_channels, cells), jnp.float32)
    pieces = []
    for offset_a in range(3):
        for offset_b in range(3):
            for offset_c in range(3):
                number = 9 * offset_a + 3 * offset_b + offset_c
                shifted = padded[:, 2 - offset_a:2 - offset_a + NX, 2 - offset_b:2 - offset_b + NY, 2 - offset_c:2 - offset_c + NZ].reshape(out_channels, cells)
                weights = kernel[:, number * in_channels:(number + 1) * in_channels]
                total = total + lax.dot_general(weights, shifted, (((0,), (0,)), ((), ())), preferred_element_type=jnp.float32)
                pieces.append(lax.dot_general(shifted, flat_activ, (((1,), (1,)), ((), ())), preferred_element_type=jnp.float32))
    grad_in = total.astype(jnp.bfloat16).reshape(in_channels, NX, NY, NZ)
    return (grad_in, jnp.concatenate(pieces, axis=1))

def reference(activations, grad_out, kernel):
    grad_input, partial_sums = lax.map(lambda pair: one_sample(pair, kernel), (activations, grad_out))
    scale_factor = 1.0 / math.sqrt(SAMPLES * NX * NY * NZ)
    grad_kernel = lax.optimization_barrier(jnp.sum(partial_sums, axis=0)) * scale_factor
    return (grad_input, grad_kernel)
```

```python
import math

import jax
import jax.numpy as jnp
from jax import lax
from jax.experimental import pallas as pl
from jax.experimental.pallas import tpu as pltpu
from jax.sharding import Mesh, PartitionSpec as P

LANES = 128
CH = 64
NX = 4
NY = 4
CELLS = NX * NY * LANES
F32 = jnp.float32
BF16 = jnp.bfloat16
ROWS = 3 * CH


def plane(ref, index):
    return ref[:, index * LANES : (index + 1) * LANES]


def shift_z(x, by):
    lane = lax.broadcasted_iota(jnp.int32, x.shape, 1)
    if by == 1:
        return jnp.where(lane == 0, 0.0, pltpu.roll(x, 1, 1))
    return jnp.where(lane == LANES - 1, 0.0, pltpu.roll(x, LANES - 1, 1))


def collect_z(t):
    return shift_z(t[0:CH], -1) + t[CH : 2 * CH] + shift_z(t[2 * CH : ROWS], 1)


def over_x(get, y):
    return [
        jnp.concatenate([get(x - (a - 1), y) for x in range(NX)], axis=1) for a in range(3)
    ]


def dot_nt(x, y):
    return lax.dot_general(x, y, (((1,), (1,)), ((), ())), preferred_element_type=F32)


def inner_kernel(g_ref, a_ref, below_ref, above_ref, w_ref, gk_ref, gi_ref, edge_ref, a3_ref):
    def get(x, y):
        if x < 0:
            return plane(below_ref, y)
        if x >= NX:
            return plane(above_ref, y)
        return plane(g_ref, x * NY + y)

    for y in range(NY):
        for x in range(NX):
            cells = plane(a_ref, x * NY + y).astype(F32)
            a3_ref[:, x * LANES : (x + 1) * LANES] = jnp.concatenate(
                [shift_z(cells, 1), cells, shift_z(cells, -1)], axis=0
            ).astype(BF16)
        if y == 0:
            edge_ref[:, 0 : NX * LANES] = a3_ref[...]
        if y == NY - 1:
            edge_ref[:, NX * LANES : 2 * NX * LANES] = a3_ref[...]
        taps = [b for b in range(3) if 0 <= y - (b - 1) < NY]
        rows = []
        for b in taps:
            rows += over_x(get, y - (b - 1))
        stack = jnp.concatenate(rows, axis=0)
        first, last = (taps[0] * ROWS, (taps[-1] + 1) * ROWS)
        terms = dot_nt(stack, a3_ref[...])
        if y == 0:
            gk_ref[first:last, :] = terms
            gk_ref[last:, :] = jnp.zeros((3 * ROWS - last, ROWS), F32)
        else:
            gk_ref[first:last, :] += terms
        t = jnp.dot(w_ref[:, first:last], stack, preferred_element_type=F32)
        for x in range(NX):
            lanes = (x * NY + y) * LANES
            gi_ref[:, lanes : lanes + LANES] = collect_z(t[:, x * LANES : (x + 1) * LANES])


def outer_kernel(
    gk_ref, gi_ref, edge_ref, w_ref, low_rim_ref, low_mid_ref, high_rim_ref, high_mid_ref,
    below_ref, above_ref, msg_ref, out_ref, wide_ref,
):
    def get(x, y):
        side = 0 if y < 0 else 1
        if x < 0:
            return plane(below_ref, side)
        if x >= NX:
            return plane(above_ref, side)
        rim, mid = ((low_rim_ref, low_mid_ref), (high_rim_ref, high_mid_ref))[side]
        if x == 0 or x == NX - 1:
            return plane(rim, x // (NX - 1))
        return plane(mid, x - 1)

    low = jnp.concatenate(over_x(get, -1), axis=0)
    high = jnp.concatenate(over_x(get, NY), axis=0)
    half = NX * LANES
    of_low = gk_ref[2 * ROWS : 3 * ROWS, :] + dot_nt(low, edge_ref[:, 0:half])
    of_high = gk_ref[0:ROWS, :] + dot_nt(high, edge_ref[:, half : 2 * half])

    def block(a, b):
        if b == 0:
            return of_high[a * CH : (a + 1) * CH]
        if b == 2:
            return of_low[a * CH : (a + 1) * CH]
        return gk_ref[ROWS + a * CH : ROWS + (a + 1) * CH, :]

    pad = jnp.zeros((CH, 2 * LANES - ROWS), F32)
    lane = lax.broadcasted_iota(jnp.int32, (CH, LANES), 1)
    for m in range(5):
        even = jnp.concatenate([block(*divmod(2 * m, 3)), pad], axis=1)
        wide_ref[3 * m] = even[:, 0:LANES]
        if m == 4:
            wide_ref[3 * m + 1] = even[:, LANES:]
            wide_ref[3 * m + 2] = jnp.zeros((CH, LANES), F32)
            wide_ref[3 * m + 3] = jnp.zeros((CH, LANES), F32)
            break
        odd = jnp.concatenate([block(*divmod(2 * m + 1, 3)), pad], axis=1)
        odd = pltpu.roll(odd, CH, 1)
        wide_ref[3 * m + 1] = jnp.where(lane < CH, even[:, LANES:], odd[:, 0:LANES])
        wide_ref[3 * m + 2] = odd[:, LANES:]
    for s in range(8):
        for column in range(16):
            at = column % 4 * LANES
            msg_ref[s * 4 + column // 4, :, at : at + LANES] = wide_ref[
                column, pl.ds(s, 8, stride=8), :
            ]

    t_low = jnp.dot(w_ref[:, 2 * ROWS : 3 * ROWS], low, preferred_element_type=F32)
    t_high = jnp.dot(w_ref[:, 0:ROWS], high, preferred_element_type=F32)
    for x in range(NX):
        for y in range(NY):
            lanes = (x * NY + y) * LANES
            value = gi_ref[:, lanes : lanes + LANES]
            if y == 0:
                value = value + collect_z(t_low[:, x * LANES : (x + 1) * LANES])
            if y == NY - 1:
                value = value + collect_z(t_high[:, x * LANES : (x + 1) * LANES])
            out_ref[:, lanes : lanes + LANES] = value.astype(BF16)


def call(body, out_shape, scratch):
    return pl.pallas_call(
        body,
        out_shape=out_shape,
        scratch_shapes=scratch,
        compiler_params=pltpu.CompilerParams(vmem_limit_bytes=48 * 1024 * 1024),
    )


def run_inner(*operands):
    shape = jax.ShapeDtypeStruct
    return call(
        inner_kernel,
        (
            shape((3 * ROWS, ROWS), F32),
            shape((CH, CELLS), F32),
            shape((ROWS, 2 * NX * LANES), BF16),
        ),
        [pltpu.VMEM((ROWS, NX * LANES), BF16)],
    )(*operands)


def run_outer(*operands):
    shape = jax.ShapeDtypeStruct
    return call(
        outer_kernel,
        (shape((32, 8, NX * LANES), F32), shape((CH, CELLS), BF16)),
        [pltpu.VMEM((16, CH, LANES), F32)],
    )(*operands)


def shifted_by(x, axis, by):
    count = lax.axis_size(axis)
    pairs = [(i, i + by) for i in range(count) if 0 <= i + by < count]
    return lax.ppermute(x, axis, pairs)


def local(activations, grad_out, kernel):
    py = ("y", "zhi")
    g = grad_out.reshape(CH, CELLS)

    def planes(cells):
        return jnp.concatenate([plane(g, x * NY + y) for x, y in cells], axis=1)

    low_rim = shifted_by(planes([(0, NY - 1), (NX - 1, NY - 1)]), py, 1)
    high_rim = shifted_by(planes([(0, 0), (NX - 1, 0)]), py, -1)
    low_mid = shifted_by(planes([(1, NY - 1), (2, NY - 1)]), py, 1)
    high_mid = shifted_by(planes([(1, 0), (2, 0)]), py, -1)
    below = shifted_by(g[:, 3 * NY * LANES :], "px", 1)
    above = shifted_by(g[:, : NY * LANES], "px", -1)

    a = activations.reshape(CH, CELLS)
    weights = kernel.reshape(CH, 3, 3, ROWS).transpose(3, 2, 1, 0).reshape(ROWS, 3 * ROWS)
    inner = run_inner(g, a, below, above, weights)
    low_rim, high_rim, *inner = lax.optimization_barrier((low_rim, high_rim, *inner))
    corner_below = shifted_by(jnp.concatenate([plane(low_rim, 1), plane(high_rim, 1)], axis=1), "px", 1)
    corner_above = shifted_by(jnp.concatenate([plane(low_rim, 0), plane(high_rim, 0)], axis=1), "px", -1)
    message, grad_input = run_outer(
        *inner, weights, low_rim, low_mid, high_rim, high_mid, corner_below, corner_above
    )

    parts = lax.all_to_all(message, ("core", "px", "y"), 0, 0)
    mine = jnp.sum(parts, axis=0).reshape(8, 1, 4, LANES)
    parts = lax.all_to_all(
        jnp.broadcast_to(mine, (8, 4, 4, LANES)).reshape(32, 4, LANES), ("zlo", "zhi"), 0, 0
    )
    mine = jnp.sum(parts, axis=0)
    parts = lax.all_to_all(jnp.broadcast_to(mine, (16, 4, LANES)), ("px", "y"), 0, 0)
    whole = parts.reshape(4, 16 * LANES)[:, : 9 * ROWS]
    total = 16 * 16 * 64 * 128
    return grad_input.reshape(1, CH, NX, NY, LANES), whole * (1.0 / math.sqrt(total))


def solution(mesh):
    axes = ("zlo", "core", "px", "y", "zhi")
    fine = Mesh(mesh.devices.reshape(8, 2, 4, 4, 4), axes)
    dp, py = ("zlo", "core"), ("y", "zhi")
    cells = P(dp, None, "px", py, None)
    return jax.shard_map(
        local, mesh=fine, in_specs=(cells, cells, P()), out_specs=(cells, P(dp, None)), check_vma=False
    )
```

```python
import math

import jax
import jax.numpy as jnp
from jax import lax
from jax.experimental import pallas as pl
from jax.experimental.pallas import tpu as pltpu
from jax.sharding import Mesh, PartitionSpec as P

LANES = 128
CH = 64
NX = 4
NY = 4
CELLS = NX * NY * LANES
F32 = jnp.float32
BF16 = jnp.bfloat16
ROWS = 3 * CH
HALF = NX * LANES
WIDE = (NX + 2) * LANES


def plane(ref, index):
    return ref[:, index * LANES : (index + 1) * LANES]


def shift_z(x, by):
    lane = lax.broadcasted_iota(jnp.int32, x.shape, 1)
    if by == 1:
        return jnp.where(lane == 0, 0.0, pltpu.roll(x, 1, 1))
    return jnp.where(lane == LANES - 1, 0.0, pltpu.roll(x, LANES - 1, 1))


def collect_z(t):
    return shift_z(t[0:CH], -1) + t[CH : 2 * CH] + shift_z(t[2 * CH : ROWS], 1)


def over_x(get, y):
    return [
        jnp.concatenate([get(x - (a - 1), y) for x in range(NX)], axis=1) for a in range(3)
    ]


def dot_nt(x, y):
    return lax.dot_general(x, y, (((1,), (1,)), ((), ())), preferred_element_type=F32)


def all_shifts(cells):
    cells = cells.astype(F32)
    return jnp.concatenate([shift_z(cells, 1), cells, shift_z(cells, -1)], axis=0).astype(BF16)


def inner_kernel(g_ref, a_ref, gk_ref, row_ref, column_ref, a3_ref):
    def get(x, y):
        if x < 0 or x >= NX:
            return jnp.zeros((CH, LANES), BF16)
        return plane(g_ref, x * NY + y)

    for y in range(NY):
        for x in range(NX):
            a3_ref[:, x * LANES : (x + 1) * LANES] = all_shifts(plane(a_ref, x * NY + y))
        if y in (0, NY - 1):
            at = y // (NY - 1) * HALF
            row_ref[:, at : at + HALF] = a3_ref[...]
        for side in range(2):
            at = side * HALF + y * LANES
            column_ref[:, at : at + LANES] = plane(a3_ref, side * (NX - 1))
        taps = [b for b in range(3) if 0 <= y - (b - 1) < NY]
        rows = []
        for b in taps:
            rows += over_x(get, y - (b - 1))
        first, last = (taps[0] * ROWS, (taps[-1] + 1) * ROWS)
        terms = dot_nt(jnp.concatenate(rows, axis=0), a3_ref[...])
        if y == 0:
            gk_ref[first:last, :] = terms
            gk_ref[last:, :] = jnp.zeros((3 * ROWS - last, ROWS), F32)
        else:
            gk_ref[first:last, :] += terms


def message_kernel(
    gk_ref, row_ref, column_ref, below_ref, above_ref, low_ref, high_ref, msg_ref, wide_ref, rim_ref
):
    for side in range(2):
        at = side * WIDE
        rim_ref[:, at : at + LANES] = all_shifts(plane(below_ref, NY + side))
        rim_ref[:, at + LANES : at + LANES + HALF] = row_ref[:, side * HALF : (side + 1) * HALF]
        rim_ref[:, at + LANES + HALF : at + WIDE] = all_shifts(plane(above_ref, NY + side))

    def block(a, b):
        value = gk_ref[b * ROWS + a * CH : b * ROWS + (a + 1) * CH, :]
        if a != 1:
            face, side = (above_ref, 1) if a == 0 else (below_ref, 0)
            rows = [y for y in range(NY) if 0 <= y - (b - 1) < NY]
            of_g = (rows[0] - (b - 1)) * LANES
            of_a = side * HALF + rows[0] * LANES
            size = len(rows) * LANES
            value = value + dot_nt(face[:, of_g : of_g + size], column_ref[:, of_a : of_a + size])
        if b != 1:
            face, side = (high_ref, 1) if b == 0 else (low_ref, 0)
            at = side * WIDE + a * LANES
            value = value + dot_nt(face[...], rim_ref[:, at : at + HALF])
        return value

    pad = jnp.zeros((CH, 2 * LANES - ROWS), F32)
    lane = lax.broadcasted_iota(jnp.int32, (CH, LANES), 1)
    for m in range(5):
        even = jnp.concatenate([block(*divmod(2 * m, 3)), pad], axis=1)
        wide_ref[3 * m] = even[:, 0:LANES]
        if m == 4:
            wide_ref[3 * m + 1] = even[:, LANES:]
            wide_ref[3 * m + 2] = jnp.zeros((CH, LANES), F32)
            wide_ref[3 * m + 3] = jnp.zeros((CH, LANES), F32)
            break
        odd = jnp.concatenate([block(*divmod(2 * m + 1, 3)), pad], axis=1)
        odd = pltpu.roll(odd, CH, 1)
        wide_ref[3 * m + 1] = jnp.where(lane < CH, even[:, LANES:], odd[:, 0:LANES])
        wide_ref[3 * m + 2] = odd[:, LANES:]
    for s in range(8):
        for column in range(16):
            at = column % 4 * LANES
            msg_ref[s * 4 + column // 4, :, at : at + LANES] = wide_ref[
                column, pl.ds(s, 8, stride=8), :
            ]


def input_kernel(
    g_ref, w_ref, below_ref, above_ref, low_ref, high_ref, corner_below_ref, corner_above_ref, out_ref
):
    def get(x, y):
        if 0 <= y < NY:
            if x < 0:
                return plane(below_ref, y)
            if x >= NX:
                return plane(above_ref, y)
            return plane(g_ref, x * NY + y)
        side = 0 if y < 0 else 1
        if x < 0:
            return plane(corner_below_ref, side)
        if x >= NX:
            return plane(corner_above_ref, side)
        return plane((low_ref, high_ref)[side], x)

    for y in range(NY):
        rows = []
        for b in range(3):
            rows += over_x(get, y - (b - 1))
        t = jnp.dot(w_ref[...], jnp.concatenate(rows, axis=0), preferred_element_type=F32)
        for x in range(NX):
            lanes = (x * NY + y) * LANES
            out_ref[:, lanes : lanes + LANES] = collect_z(
                t[:, x * LANES : (x + 1) * LANES]
            ).astype(BF16)


def call(body, out_shape, scratch=(), cost=None):
    return pl.pallas_call(
        body,
        out_shape=out_shape,
        scratch_shapes=scratch,
        cost_estimate=cost,
        compiler_params=pltpu.CompilerParams(vmem_limit_bytes=48 * 1024 * 1024),
    )


def run_inner(*operands):
    shape = jax.ShapeDtypeStruct
    return call(
        inner_kernel,
        (shape((3 * ROWS, ROWS), F32), shape((ROWS, 2 * HALF), BF16), shape((ROWS, 2 * HALF), BF16)),
        [pltpu.VMEM((ROWS, HALF), BF16)],
        pl.CostEstimate(flops=20 * 10**9, transcendentals=0, bytes_accessed=2**20),
    )(*operands)


def run_message(*operands):
    return call(
        message_kernel,
        jax.ShapeDtypeStruct((32, 8, HALF), F32),
        [pltpu.VMEM((16, CH, LANES), F32), pltpu.VMEM((ROWS, 2 * WIDE), BF16)],
    )(*operands)


def run_input(*operands):
    return call(input_kernel, jax.ShapeDtypeStruct((CH, CELLS), BF16))(*operands)


def shifted_by(x, axis, by):
    count = lax.axis_size(axis)
    pairs = [(i, i + by) for i in range(count) if 0 <= i + by < count]
    return lax.ppermute(x, axis, pairs)


def local(activations, grad_out, kernel):
    py = ("y", "zhi")
    g = grad_out.reshape(CH, CELLS)

    def planes(cells):
        return jnp.concatenate([plane(g, x * NY + y) for x, y in cells], axis=1)

    low = shifted_by(planes([(x, NY - 1) for x in range(NX)]), py, 1)
    high = shifted_by(planes([(x, 0) for x in range(NX)]), py, -1)

    a = activations.reshape(CH, CELLS)

    weights = kernel.reshape(CH, 3, 3, ROWS).transpose(3, 2, 1, 0).reshape(ROWS, 3 * ROWS)

    def x_face(x):
        rows = g[:, x * NY * LANES : (x + 1) * NY * LANES]
        return jnp.concatenate([rows, plane(a, x * NY), plane(a, x * NY + NY - 1)], axis=1)

    below = shifted_by(x_face(NX - 1), "px", 1)
    above = shifted_by(x_face(0), "px", -1)
    inner = run_inner(g, a)
    weights, *inner = lax.optimization_barrier((weights, *inner))
    message = run_message(*inner, below, above, low, high)

    parts = lax.all_to_all(message, ("core", "px", "y"), 0, 0)
    mine = jnp.sum(parts, axis=0).reshape(8, 1, 4, LANES)
    mine, low, high = lax.optimization_barrier((mine, low, high))
    parts = lax.all_to_all(
        jnp.broadcast_to(mine, (8, 4, 4, LANES)).reshape(32, 4, LANES), ("zlo", "zhi"), 0, 0
    )
    last = (NX - 1) * LANES
    corner_below = shifted_by(jnp.concatenate([low[:, last:], high[:, last:]], axis=1), "px", 1)
    corner_above = shifted_by(jnp.concatenate([plane(low, 0), plane(high, 0)], axis=1), "px", -1)
    grad_input = run_input(g, weights, below, above, low, high, corner_below, corner_above)
    parts, grad_input = lax.optimization_barrier((parts, grad_input))
    mine = jnp.sum(parts, axis=0)
    parts = lax.all_to_all(jnp.broadcast_to(mine, (16, 4, LANES)), ("px", "y"), 0, 0)
    whole = parts.reshape(4, 16 * LANES)[:, : 9 * ROWS]
    total = 16 * 16 * 64 * 128
    return grad_input.reshape(1, CH, NX, NY, LANES), whole * (1.0 / math.sqrt(total))


def solution(mesh):
    axes = ("zlo", "core", "px", "y", "zhi")
    fine = Mesh(mesh.devices.reshape(8, 2, 4, 4, 4), axes)
    dp, py = ("zlo", "core"), ("y", "zhi")
    cells = P(dp, None, "px", py, None)
    return jax.shard_map(
        local, mesh=fine, in_specs=(cells, cells, P()), out_specs=(cells, P(dp, None)), check_vma=False
    )
```

```python
import math

import jax
import jax.numpy as jnp
from jax import lax
from jax.experimental import pallas as pl
from jax.experimental.pallas import tpu as pltpu
from jax.sharding import Mesh, PartitionSpec as P

LANES = 128
CH = 64
NX = 4
NY = 4
CELLS = NX * NY * LANES
F32 = jnp.float32
BF16 = jnp.bfloat16
ROWS = 3 * CH
HALF = NX * LANES
WIDE = (NX + 2) * LANES


def plane(ref, index):
    return ref[:, index * LANES : (index + 1) * LANES]


def shift_z(x, by):
    lane = lax.broadcasted_iota(jnp.int32, x.shape, 1)
    if by == 1:
        return jnp.where(lane == 0, 0.0, pltpu.roll(x, 1, 1))
    return jnp.where(lane == LANES - 1, 0.0, pltpu.roll(x, LANES - 1, 1))


def collect_z(t):
    return shift_z(t[0:CH], -1) + t[CH : 2 * CH] + shift_z(t[2 * CH : ROWS], 1)


def over_x(get, y):
    return [
        jnp.concatenate([get(x - (a - 1), y) for x in range(NX)], axis=1) for a in range(3)
    ]


def dot_nt(x, y):
    return lax.dot_general(x, y, (((1,), (1,)), ((), ())), preferred_element_type=F32)


def all_shifts(cells):
    cells = cells.astype(F32)
    return jnp.concatenate([shift_z(cells, 1), cells, shift_z(cells, -1)], axis=0).astype(BF16)


def inner_kernel(g_ref, a_ref, gk_ref, row_ref, column_ref, a3_ref):
    def get(x, y):
        if x < 0 or x >= NX:
            return jnp.zeros((CH, LANES), BF16)
        return plane(g_ref, x * NY + y)

    for y in range(NY):
        for x in range(NX):
            a3_ref[:, x * LANES : (x + 1) * LANES] = all_shifts(plane(a_ref, x * NY + y))
        if y in (0, NY - 1):
            at = y // (NY - 1) * HALF
            row_ref[:, at : at + HALF] = a3_ref[...]
        for side in range(2):
            at = side * HALF + y * LANES
            column_ref[:, at : at + LANES] = plane(a3_ref, side * (NX - 1))
        taps = [b for b in range(3) if 0 <= y - (b - 1) < NY]
        rows = []
        for b in taps:
            rows += over_x(get, y - (b - 1))
        first, last = (taps[0] * ROWS, (taps[-1] + 1) * ROWS)
        terms = dot_nt(jnp.concatenate(rows, axis=0), a3_ref[...])
        if y == 0:
            gk_ref[first:last, :] = terms
            gk_ref[last:, :] = jnp.zeros((3 * ROWS - last, ROWS), F32)
        else:
            gk_ref[first:last, :] += terms


def message_kernel(
    gk_ref, row_ref, column_ref, below_ref, above_ref, low_ref, high_ref, msg_ref, wide_ref, rim_ref
):
    for side in range(2):
        at = side * WIDE
        rim_ref[:, at : at + LANES] = all_shifts(plane(below_ref, NY + side))
        rim_ref[:, at + LANES : at + LANES + HALF] = row_ref[:, side * HALF : (side + 1) * HALF]
        rim_ref[:, at + LANES + HALF : at + WIDE] = all_shifts(plane(above_ref, NY + side))

    def block(a, b):
        value = gk_ref[b * ROWS + a * CH : b * ROWS + (a + 1) * CH, :]
        if a != 1:
            face, side = (above_ref, 1) if a == 0 else (below_ref, 0)
            rows = [y for y in range(NY) if 0 <= y - (b - 1) < NY]
            of_g = (rows[0] - (b - 1)) * LANES
            of_a = side * HALF + rows[0] * LANES
            size = len(rows) * LANES
            value = value + dot_nt(face[:, of_g : of_g + size], column_ref[:, of_a : of_a + size])
        if b != 1:
            face, side = (high_ref, 1) if b == 0 else (low_ref, 0)
            at = side * WIDE + a * LANES
            value = value + dot_nt(face[...], rim_ref[:, at : at + HALF])
        return value

    pad = jnp.zeros((CH, 2 * LANES - ROWS), F32)
    lane = lax.broadcasted_iota(jnp.int32, (CH, LANES), 1)
    for m in range(5):
        even = jnp.concatenate([block(*divmod(2 * m, 3)), pad], axis=1)
        wide_ref[3 * m] = even[:, 0:LANES]
        if m == 4:
            wide_ref[3 * m + 1] = even[:, LANES:]
            wide_ref[3 * m + 2] = jnp.zeros((CH, LANES), F32)
            wide_ref[3 * m + 3] = jnp.zeros((CH, LANES), F32)
            break
        odd = jnp.concatenate([block(*divmod(2 * m + 1, 3)), pad], axis=1)
        odd = pltpu.roll(odd, CH, 1)
        wide_ref[3 * m + 1] = jnp.where(lane < CH, even[:, LANES:], odd[:, 0:LANES])
        wide_ref[3 * m + 2] = odd[:, LANES:]
    for s in range(8):
        for column in range(16):
            at = column % 4 * LANES
            msg_ref[s * 4 + column // 4, :, at : at + LANES] = wide_ref[
                column, pl.ds(s, 8, stride=8), :
            ]


def input_kernel(
    g_ref, w_ref, below_ref, above_ref, low_ref, high_ref, corner_below_ref, corner_above_ref, out_ref
):
    def get(x, y):
        if 0 <= y < NY:
            if x < 0:
                return plane(below_ref, y)
            if x >= NX:
                return plane(above_ref, y)
            return plane(g_ref, x * NY + y)
        side = 0 if y < 0 else 1
        if x < 0:
            return plane(corner_below_ref, side)
        if x >= NX:
            return plane(corner_above_ref, side)
        return plane((low_ref, high_ref)[side], x)

    for y in range(NY):
        rows = []
        for b in range(3):
            rows += over_x(get, y - (b - 1))
        t = jnp.dot(w_ref[...], jnp.concatenate(rows, axis=0), preferred_element_type=F32)
        for x in range(NX):
            lanes = (x * NY + y) * LANES
            out_ref[:, lanes : lanes + LANES] = collect_z(
                t[:, x * LANES : (x + 1) * LANES]
            ).astype(BF16)


def call(body, out_shape, scratch=(), cost=None):
    return pl.pallas_call(
        body,
        out_shape=out_shape,
        scratch_shapes=scratch,
        cost_estimate=cost,
        compiler_params=pltpu.CompilerParams(vmem_limit_bytes=48 * 1024 * 1024),
    )


def run_inner(*operands):
    shape = jax.ShapeDtypeStruct
    return call(
        inner_kernel,
        (shape((3 * ROWS, ROWS), F32), shape((ROWS, 2 * HALF), BF16), shape((ROWS, 2 * HALF), BF16)),
        [pltpu.VMEM((ROWS, HALF), BF16)],
        pl.CostEstimate(flops=20 * 10**9, transcendentals=0, bytes_accessed=2**20),
    )(*operands)


def run_message(*operands):
    return call(
        message_kernel,
        jax.ShapeDtypeStruct((32, 8, HALF), F32),
        [pltpu.VMEM((16, CH, LANES), F32), pltpu.VMEM((ROWS, 2 * WIDE), BF16)],
    )(*operands)


def run_input(*operands):
    return call(input_kernel, jax.ShapeDtypeStruct((CH, CELLS), BF16))(*operands)


def shifted_by(x, axis, by):
    count = lax.axis_size(axis)
    pairs = [(i, i + by) for i in range(count) if 0 <= i + by < count]
    return lax.ppermute(x, axis, pairs)


def local(activations, grad_out, kernel):
    py = ("y", "zhi")
    g = grad_out.reshape(CH, CELLS)

    def planes(cells):
        return jnp.concatenate([plane(g, x * NY + y) for x, y in cells], axis=1)

    low = shifted_by(planes([(x, NY - 1) for x in range(NX)]), py, 1)
    high = shifted_by(planes([(x, 0) for x in range(NX)]), py, -1)

    a = activations.reshape(CH, CELLS)

    weights = kernel.reshape(CH, 3, 3, ROWS).transpose(3, 2, 1, 0).reshape(ROWS, 3 * ROWS)

    def x_face(x):
        rows = g[:, x * NY * LANES : (x + 1) * NY * LANES]
        return jnp.concatenate([rows, plane(a, x * NY), plane(a, x * NY + NY - 1)], axis=1)

    below = shifted_by(x_face(NX - 1), "px", 1)
    above = shifted_by(x_face(0), "px", -1)
    inner = run_inner(g, a)
    weights, *inner = lax.optimization_barrier((weights, *inner))
    message = run_message(*inner, below, above, low, high)

    parts = lax.all_to_all(message, ("core", "px", "y"), 0, 0)
    mine = jnp.sum(parts, axis=0).reshape(8, 4, LANES)
    mine, low, high = lax.optimization_barrier((mine, low, high))
    parts = lax.all_to_all(mine, "zlo", 0, 0)
    last = (NX - 1) * LANES
    corner_below = shifted_by(jnp.concatenate([low[:, last:], high[:, last:]], axis=1), "px", 1)
    corner_above = shifted_by(jnp.concatenate([plane(low, 0), plane(high, 0)], axis=1), "px", -1)
    parts, corner_below, corner_above = lax.optimization_barrier((parts, corner_below, corner_above))
    mine = jnp.sum(parts, axis=0)
    parts = lax.all_to_all(jnp.broadcast_to(mine, (4, 4, LANES)), "zhi", 0, 0)
    grad_input = run_input(g, weights, below, above, low, high, corner_below, corner_above)
    parts, grad_input = lax.optimization_barrier((parts, grad_input))
    total = 16 * 16 * 64 * 128
    mine = jnp.sum(parts, axis=0) * (1.0 / math.sqrt(total))
    parts = lax.all_to_all(jnp.broadcast_to(mine, (16, 4, LANES)), ("px", "y"), 0, 0)
    whole = parts.reshape(4, 16 * LANES)[:, : 9 * ROWS]
    return grad_input.reshape(1, CH, NX, NY, LANES), whole


def solution(mesh):
    axes = ("zlo", "core", "px", "y", "zhi")
    fine = Mesh(mesh.devices.reshape(8, 2, 4, 4, 4), axes)
    dp, py = ("zlo", "core"), ("y", "zhi")
    cells = P(dp, None, "px", py, None)
    return jax.shard_map(
        local, mesh=fine, in_specs=(cells, cells, P()), out_specs=(cells, P(dp, None)), check_vma=False
    )
```

```python
import math

import jax
import jax.numpy as jnp
from jax import lax
from jax.experimental import pallas as pl
from jax.experimental.pallas import tpu as pltpu
from jax.sharding import Mesh, PartitionSpec as P

LANES = 128
CH = 64
NX = 4
NY = 4
CELLS = NX * NY * LANES
F32 = jnp.float32
BF16 = jnp.bfloat16
ROWS = 3 * CH
HALF = NX * LANES
WIDE = (NX + 2) * LANES


def plane(ref, index):
    return ref[:, index * LANES : (index + 1) * LANES]


def shift_z(x, by):
    lane = lax.broadcasted_iota(jnp.int32, x.shape, 1)
    if by == 1:
        return jnp.where(lane == 0, 0.0, pltpu.roll(x, 1, 1))
    return jnp.where(lane == LANES - 1, 0.0, pltpu.roll(x, LANES - 1, 1))


def collect_z(t):
    return shift_z(t[0:CH], -1) + t[CH : 2 * CH] + shift_z(t[2 * CH : ROWS], 1)


def over_x(get, y):
    return [
        jnp.concatenate([get(x - (a - 1), y) for x in range(NX)], axis=1) for a in range(3)
    ]


def dot_nt(x, y):
    return lax.dot_general(x, y, (((1,), (1,)), ((), ())), preferred_element_type=F32)


def all_shifts(cells):
    cells = cells.astype(F32)
    return jnp.concatenate([shift_z(cells, 1), cells, shift_z(cells, -1)], axis=0).astype(BF16)


def inner_kernel(g_ref, a_ref, gk_ref, row_ref, column_ref, a3_ref):
    def get(x, y):
        if x < 0 or x >= NX:
            return jnp.zeros((CH, LANES), BF16)
        return plane(g_ref, x * NY + y)

    for y in range(NY):
        for x in range(NX):
            a3_ref[:, x * LANES : (x + 1) * LANES] = all_shifts(plane(a_ref, x * NY + y))
        if y in (0, NY - 1):
            at = y // (NY - 1) * HALF
            row_ref[:, at : at + HALF] = a3_ref[...]
        for side in range(2):
            at = side * HALF + y * LANES
            column_ref[:, at : at + LANES] = plane(a3_ref, side * (NX - 1))
        taps = [b for b in range(3) if 0 <= y - (b - 1) < NY]
        rows = []
        for b in taps:
            rows += over_x(get, y - (b - 1))
        first, last = (taps[0] * ROWS, (taps[-1] + 1) * ROWS)
        terms = dot_nt(jnp.concatenate(rows, axis=0), a3_ref[...])
        if y == 0:
            gk_ref[first:last, :] = terms
            gk_ref[last:, :] = jnp.zeros((3 * ROWS - last, ROWS), F32)
        else:
            gk_ref[first:last, :] += terms


def message_kernel(
    core_ref, g_ref, gk_ref, row_ref, column_ref, below_ref, above_ref, far_ref, msg_ref, wide_ref, rim_ref, far3_ref
):
    upward = core_ref[0] == 0

    def near(low, high):
        return jnp.where(upward, low, high)

    rim_ref[:, 0:LANES] = all_shifts(near(plane(below_ref, NY), plane(below_ref, NY + 1)))
    rim_ref[:, LANES : LANES + HALF] = near(row_ref[:, 0:HALF], row_ref[:, HALF : 2 * HALF])
    rim_ref[:, LANES + HALF : WIDE] = all_shifts(near(plane(above_ref, NY), plane(above_ref, NY + 1)))
    for x in range(NX):
        far3_ref[:, x * LANES : (x + 1) * LANES] = all_shifts(plane(far_ref, NX + x))
    own = [near(plane(below_ref, 0), plane(below_ref, NY - 1))]
    own += [near(plane(g_ref, x * NY), plane(g_ref, x * NY + NY - 1)) for x in range(NX)]
    own += [near(plane(above_ref, 0), plane(above_ref, NY - 1))]

    def across(a):
        of_far = dot_nt(far_ref[:, 0:HALF], rim_ref[:, a * LANES : a * LANES + HALF])
        of_own = dot_nt(jnp.concatenate(own[2 - a : 2 - a + NX], axis=1), far3_ref[...])
        return jnp.where(upward, of_own, of_far), jnp.where(upward, of_far, of_own)

    pairs = [across(a) for a in range(3)]

    def block(a, b):
        value = gk_ref[b * ROWS + a * CH : b * ROWS + (a + 1) * CH, :]
        if a != 1:
            face, side = (above_ref, 1) if a == 0 else (below_ref, 0)
            rows = [y for y in range(NY) if 0 <= y - (b - 1) < NY]
            of_g = (rows[0] - (b - 1)) * LANES
            of_a = side * HALF + rows[0] * LANES
            size = len(rows) * LANES
            value = value + dot_nt(face[:, of_g : of_g + size], column_ref[:, of_a : of_a + size])
        if b != 1:
            value = value + pairs[a][b // 2]
        return value

    pad = jnp.zeros((CH, 2 * LANES - ROWS), F32)
    lane = lax.broadcasted_iota(jnp.int32, (CH, LANES), 1)
    for m in range(5):
        even = jnp.concatenate([block(*divmod(2 * m, 3)), pad], axis=1)
        wide_ref[3 * m] = even[:, 0:LANES]
        if m == 4:
            wide_ref[3 * m + 1] = even[:, LANES:]
            wide_ref[3 * m + 2] = jnp.zeros((CH, LANES), F32)
            wide_ref[3 * m + 3] = jnp.zeros((CH, LANES), F32)
            break
        odd = jnp.concatenate([block(*divmod(2 * m + 1, 3)), pad], axis=1)
        odd = pltpu.roll(odd, CH, 1)
        wide_ref[3 * m + 1] = jnp.where(lane < CH, even[:, LANES:], odd[:, 0:LANES])
        wide_ref[3 * m + 2] = odd[:, LANES:]
    for s in range(8):
        for column in range(16):
            at = column % 4 * LANES
            msg_ref[s * 4 + column // 4, :, at : at + LANES] = wide_ref[
                column, pl.ds(s, 8, stride=8), :
            ]


def input_kernel(
    g_ref, w_ref, below_ref, above_ref, low_ref, high_ref, corner_below_ref, corner_above_ref, out_ref
):
    def get(x, y):
        if 0 <= y < NY:
            if x < 0:
                return plane(below_ref, y)
            if x >= NX:
                return plane(above_ref, y)
            return plane(g_ref, x * NY + y)
        side = 0 if y < 0 else 1
        if x < 0:
            return plane(corner_below_ref, side)
        if x >= NX:
            return plane(corner_above_ref, side)
        return plane((low_ref, high_ref)[side], x)

    for y in range(NY):
        rows = []
        for b in range(3):
            rows += over_x(get, y - (b - 1))
        t = jnp.dot(w_ref[...], jnp.concatenate(rows, axis=0), preferred_element_type=F32)
        for x in range(NX):
            lanes = (x * NY + y) * LANES
            out_ref[:, lanes : lanes + LANES] = collect_z(
                t[:, x * LANES : (x + 1) * LANES]
            ).astype(BF16)


def call(body, out_shape, scratch=(), cost=None, **specs):
    return pl.pallas_call(
        body,
        out_shape=out_shape,
        scratch_shapes=scratch,
        cost_estimate=cost,
        compiler_params=pltpu.CompilerParams(vmem_limit_bytes=48 * 1024 * 1024),
        **specs,
    )


def run_inner(*operands):
    shape = jax.ShapeDtypeStruct
    return call(
        inner_kernel,
        (shape((3 * ROWS, ROWS), F32), shape((ROWS, 2 * HALF), BF16), shape((ROWS, 2 * HALF), BF16)),
        [pltpu.VMEM((ROWS, HALF), BF16)],
        pl.CostEstimate(flops=20 * 10**9, transcendentals=0, bytes_accessed=2**20),
    )(*operands)


def run_message(core, *operands):
    vmem = pl.BlockSpec(memory_space=pltpu.VMEM)
    return call(
        message_kernel,
        jax.ShapeDtypeStruct((32, 8, HALF), F32),
        [
            pltpu.VMEM((16, CH, LANES), F32),
            pltpu.VMEM((ROWS, WIDE), BF16),
            pltpu.VMEM((ROWS, HALF), BF16),
        ],
        in_specs=[pl.BlockSpec(memory_space=pltpu.SMEM)] + [vmem] * len(operands),
        out_specs=vmem,
    )(core.reshape(1), *operands)


def run_input(*operands):
    return call(input_kernel, jax.ShapeDtypeStruct((CH, CELLS), BF16))(*operands)


def shifted_by(x, axis, by):
    count = lax.axis_size(axis)
    pairs = [(i, i + by) for i in range(count) if 0 <= i + by < count]
    return lax.ppermute(x, axis, pairs)


def along_y(x, by):
    count = lax.axis_size("y") * lax.axis_size("zhi")
    pairs = []
    for core, step in enumerate((by, -by)):
        pairs += [(core * count + i, core * count + i + step) for i in range(count) if 0 <= i + step < count]
    return lax.ppermute(x, ("core", "y", "zhi"), pairs)


def local(activations, grad_out, kernel):
    core = lax.axis_index("core")
    g = grad_out.reshape(CH, CELLS)
    a = activations.reshape(CH, CELLS)

    def rows(cells, y):
        return jnp.concatenate([plane(cells, x * NY + y) for x in range(NX)], axis=1)

    g_low, g_high = rows(g, 0), rows(g, NY - 1)
    ahead = jnp.where(core == 0, g_high, g_low)
    ahead = jnp.concatenate([ahead, jnp.where(core == 0, rows(a, NY - 1), rows(a, 0))], axis=1)
    far = along_y(ahead, 1)
    back = along_y(jnp.where(core == 0, g_low, g_high), -1)


    weights = kernel.reshape(CH, 3, 3, ROWS).transpose(3, 2, 1, 0).reshape(ROWS, 3 * ROWS)

    def x_face(x):
        cells = g[:, x * NY * LANES : (x + 1) * NY * LANES]
        return jnp.concatenate([cells, plane(a, x * NY), plane(a, x * NY + NY - 1), cells[:, LANES:]], axis=1)

    below = shifted_by(x_face(NX - 1), "px", 1)
    above = shifted_by(x_face(0), "px", -1)
    inner = run_inner(g, a)
    weights, *inner = lax.optimization_barrier((weights, *inner))
    message = run_message(core, g, *inner, below, above, far)

    parts = lax.all_to_all(message, ("core", "px", "y"), 0, 0)
    mine = jnp.sum(parts, axis=0).reshape(8, 1, 4, LANES)
    mine, far = lax.optimization_barrier((mine, far))
    low = jnp.where(core == 0, far[:, :HALF], back)
    high = jnp.where(core == 0, back, far[:, :HALF])
    parts = lax.all_to_all(
        jnp.broadcast_to(mine, (8, 4, 4, LANES)).reshape(32, 4, LANES), ("zlo", "zhi"), 0, 0
    )
    last = (NX - 1) * LANES
    corner_below = shifted_by(jnp.concatenate([low[:, last:], high[:, last:]], axis=1), "px", 1)
    corner_above = shifted_by(jnp.concatenate([plane(low, 0), plane(high, 0)], axis=1), "px", -1)
    grad_input = run_input(g, weights, below, above, low, high, corner_below, corner_above)
    parts, grad_input = lax.optimization_barrier((parts, grad_input))
    mine = jnp.sum(parts, axis=0)
    parts = lax.all_to_all(jnp.broadcast_to(mine, (16, 4, LANES)), ("px", "y"), 0, 0)
    whole = parts.reshape(4, 16 * LANES)[:, : 9 * ROWS]
    total = 16 * 16 * 64 * 128
    return grad_input.reshape(1, CH, NX, NY, LANES), whole * (1.0 / math.sqrt(total))


def solution(mesh):
    axes = ("zlo", "core", "px", "y", "zhi")
    fine = Mesh(mesh.devices.reshape(8, 2, 4, 4, 4), axes)
    dp, py = ("zlo", "core"), ("y", "zhi")
    cells = P(dp, None, "px", py, None)
    return jax.shard_map(
        local, mesh=fine, in_specs=(cells, cells, P()), out_specs=(cells, P(dp, None)), check_vma=False
    )
```

```python
import math

import jax
import jax.numpy as jnp
import numpy as np
from jax import lax
from jax.experimental import pallas as pl
from jax.experimental.pallas import tpu as pltpu
from jax.sharding import Mesh, PartitionSpec as P

AXES = ("zlo", "core", "px", "y", "zhi")
LANES = 128
CH = 64
NX = 4
NY = 4
CELLS = NX * NY * LANES
F32 = jnp.float32
BF16 = jnp.bfloat16
ROWS = 3 * CH
HALF = NX * LANES
WIDE = (NX + 2) * LANES


def plane(ref, index):
    return ref[:, index * LANES : (index + 1) * LANES]


def shift_z(x, by):
    lane = lax.broadcasted_iota(jnp.int32, x.shape, 1)
    if by == 1:
        return jnp.where(lane == 0, 0.0, pltpu.roll(x, 1, 1))
    return jnp.where(lane == LANES - 1, 0.0, pltpu.roll(x, LANES - 1, 1))


def collect_z(t):
    return shift_z(t[0:CH], -1) + t[CH : 2 * CH] + shift_z(t[2 * CH : ROWS], 1)


def over_x(get, y):
    return [
        jnp.concatenate([get(x - (a - 1), y) for x in range(NX)], axis=1) for a in range(3)
    ]


def dot_nt(x, y):
    return lax.dot_general(x, y, (((1,), (1,)), ((), ())), preferred_element_type=F32)


def all_shifts(cells):
    cells = cells.astype(F32)
    return jnp.concatenate([shift_z(cells, 1), cells, shift_z(cells, -1)], axis=0).astype(BF16)


def inner_kernel(g_ref, a_ref, gk_ref, row_ref, column_ref, a3_ref):
    def get(x, y):
        if x < 0 or x >= NX:
            return jnp.zeros((CH, LANES), BF16)
        return plane(g_ref, x * NY + y)

    for y in range(NY):
        for x in range(NX):
            a3_ref[:, x * LANES : (x + 1) * LANES] = all_shifts(plane(a_ref, x * NY + y))
        if y in (0, NY - 1):
            at = y // (NY - 1) * HALF
            row_ref[:, at : at + HALF] = a3_ref[...]
        for side in range(2):
            at = side * HALF + y * LANES
            column_ref[:, at : at + LANES] = plane(a3_ref, side * (NX - 1))
        taps = [b for b in range(3) if 0 <= y - (b - 1) < NY]
        rows = []
        for b in taps:
            rows += over_x(get, y - (b - 1))
        first, last = (taps[0] * ROWS, (taps[-1] + 1) * ROWS)
        terms = dot_nt(jnp.concatenate(rows, axis=0), a3_ref[...])
        if y == 0:
            gk_ref[first:last, :] = terms
            gk_ref[last:, :] = jnp.zeros((3 * ROWS - last, ROWS), F32)
        else:
            gk_ref[first:last, :] += terms


def message_kernel(
    core_ref, g_ref, gk_ref, row_ref, column_ref, below_ref, above_ref, far_ref, msg_ref, wide_ref, rim_ref, far3_ref
):
    upward = core_ref[0] == 0

    def near(low, high):
        return jnp.where(upward, low, high)

    rim_ref[:, 0:LANES] = all_shifts(near(plane(below_ref, NY), plane(below_ref, NY + 1)))
    rim_ref[:, LANES : LANES + HALF] = near(row_ref[:, 0:HALF], row_ref[:, HALF : 2 * HALF])
    rim_ref[:, LANES + HALF : WIDE] = all_shifts(near(plane(above_ref, NY), plane(above_ref, NY + 1)))
    for x in range(NX):
        far3_ref[:, x * LANES : (x + 1) * LANES] = all_shifts(plane(far_ref, NX + x))
    own = [near(plane(below_ref, 0), plane(below_ref, NY - 1))]
    own += [near(plane(g_ref, x * NY), plane(g_ref, x * NY + NY - 1)) for x in range(NX)]
    own += [near(plane(above_ref, 0), plane(above_ref, NY - 1))]

    def across(a):
        of_far = dot_nt(far_ref[:, 0:HALF], rim_ref[:, a * LANES : a * LANES + HALF])
        of_own = dot_nt(jnp.concatenate(own[2 - a : 2 - a + NX], axis=1), far3_ref[...])
        return jnp.where(upward, of_own, of_far), jnp.where(upward, of_far, of_own)

    pairs = [across(a) for a in range(3)]

    def block(a, b):
        value = gk_ref[b * ROWS + a * CH : b * ROWS + (a + 1) * CH, :]
        if a != 1:
            face, side = (above_ref, 1) if a == 0 else (below_ref, 0)
            rows = [y for y in range(NY) if 0 <= y - (b - 1) < NY]
            of_g = (rows[0] - (b - 1)) * LANES
            of_a = side * HALF + rows[0] * LANES
            size = len(rows) * LANES
            value = value + dot_nt(face[:, of_g : of_g + size], column_ref[:, of_a : of_a + size])
        if b != 1:
            value = value + pairs[a][b // 2]
        return value

    pad = jnp.zeros((CH, 2 * LANES - ROWS), F32)
    lane = lax.broadcasted_iota(jnp.int32, (CH, LANES), 1)
    for m in range(5):
        even = jnp.concatenate([block(*divmod(2 * m, 3)), pad], axis=1)
        wide_ref[3 * m] = even[:, 0:LANES]
        if m == 4:
            wide_ref[3 * m + 1] = even[:, LANES:]
            wide_ref[3 * m + 2] = jnp.zeros((CH, LANES), F32)
            wide_ref[3 * m + 3] = jnp.zeros((CH, LANES), F32)
            break
        odd = jnp.concatenate([block(*divmod(2 * m + 1, 3)), pad], axis=1)
        odd = pltpu.roll(odd, CH, 1)
        wide_ref[3 * m + 1] = jnp.where(lane < CH, even[:, LANES:], odd[:, 0:LANES])
        wide_ref[3 * m + 2] = odd[:, LANES:]
    for s in range(8):
        for column in range(16):
            at = column % 4 * LANES
            msg_ref[s * 4 + column // 4, :, at : at + LANES] = wide_ref[
                column, pl.ds(s, 8, stride=8), :
            ]


def input_kernel(
    g_ref, w_ref, below_ref, above_ref, low_ref, high_ref, corner_below_ref, corner_above_ref, out_ref
):
    def get(x, y):
        if 0 <= y < NY:
            if x < 0:
                return plane(below_ref, y)
            if x >= NX:
                return plane(above_ref, y)
            return plane(g_ref, x * NY + y)
        side = 0 if y < 0 else 1
        if x < 0:
            return plane(corner_below_ref, side)
        if x >= NX:
            return plane(corner_above_ref, side)
        return plane((low_ref, high_ref)[side], x)

    for y in range(NY):
        rows = []
        for b in range(3):
            rows += over_x(get, y - (b - 1))
        t = jnp.dot(w_ref[...], jnp.concatenate(rows, axis=0), preferred_element_type=F32)
        for x in range(NX):
            lanes = (x * NY + y) * LANES
            out_ref[:, lanes : lanes + LANES] = collect_z(
                t[:, x * LANES : (x + 1) * LANES]
            ).astype(BF16)


def call(body, out_shape, scratch=(), cost=None, **specs):
    return pl.pallas_call(
        body,
        out_shape=out_shape,
        scratch_shapes=scratch,
        cost_estimate=cost,
        compiler_params=pltpu.CompilerParams(vmem_limit_bytes=48 * 1024 * 1024),
        **specs,
    )


def run_inner(*operands):
    shape = jax.ShapeDtypeStruct
    return call(
        inner_kernel,
        (shape((3 * ROWS, ROWS), F32), shape((ROWS, 2 * HALF), BF16), shape((ROWS, 2 * HALF), BF16)),
        [pltpu.VMEM((ROWS, HALF), BF16)],
        pl.CostEstimate(flops=20 * 10**9, transcendentals=0, bytes_accessed=2**20),
    )(*operands)


def run_message(core, *operands):
    vmem = pl.BlockSpec(memory_space=pltpu.VMEM)
    return call(
        message_kernel,
        jax.ShapeDtypeStruct((32, 8, HALF), F32),
        [
            pltpu.VMEM((16, CH, LANES), F32),
            pltpu.VMEM((ROWS, WIDE), BF16),
            pltpu.VMEM((ROWS, HALF), BF16),
        ],
        in_specs=[pl.BlockSpec(memory_space=pltpu.SMEM)] + [vmem] * len(operands),
        out_specs=vmem,
    )(core.reshape(1), *operands)


def run_input(*operands):
    return call(input_kernel, jax.ShapeDtypeStruct((CH, CELLS), BF16))(*operands)


def shifted_by(x, axis, by):
    count = lax.axis_size(axis)
    pairs = [(i, i + by) for i in range(count) if 0 <= i + by < count]
    return lax.ppermute(x, axis, pairs)


def lines_along_z(first):
    sizes = [lax.axis_size(axis) for axis in AXES]
    place = np.arange(math.prod(sizes)).reshape(sizes)
    lines = place.transpose(1, 2, 3, 4, 0).reshape(-1, sizes[4] * sizes[0])
    return np.roll(lines, -first, axis=1).tolist()


def along_y(x, by):
    count = lax.axis_size("y") * lax.axis_size("zhi")
    pairs = []
    for core, step in enumerate((by, -by)):
        pairs += [(core * count + i, core * count + i + step) for i in range(count) if 0 <= i + step < count]
    return lax.ppermute(x, ("core", "y", "zhi"), pairs)


def local(activations, grad_out, kernel):
    core = lax.axis_index("core")
    g = grad_out.reshape(CH, CELLS)
    a = activations.reshape(CH, CELLS)

    def rows(cells, y):
        return jnp.concatenate([plane(cells, x * NY + y) for x in range(NX)], axis=1)

    g_low, g_high = rows(g, 0), rows(g, NY - 1)
    ahead = jnp.where(core == 0, g_high, g_low)
    ahead = jnp.concatenate([ahead, jnp.where(core == 0, rows(a, NY - 1), rows(a, 0))], axis=1)
    far = along_y(ahead, 1)
    back = along_y(jnp.where(core == 0, g_low, g_high), -1)


    weights = kernel.reshape(CH, 3, 3, ROWS).transpose(3, 2, 1, 0).reshape(ROWS, 3 * ROWS)

    def x_face(x):
        cells = g[:, x * NY * LANES : (x + 1) * NY * LANES]
        return jnp.concatenate([cells, plane(a, x * NY), plane(a, x * NY + NY - 1), cells[:, LANES:]], axis=1)

    below = shifted_by(x_face(NX - 1), "px", 1)
    above = shifted_by(x_face(0), "px", -1)
    inner = run_inner(g, a)
    weights, *inner = lax.optimization_barrier((weights, *inner))
    message = run_message(core, g, *inner, below, above, far)

    parts = lax.all_to_all(message, ("core", "px", "y"), 0, 0)
    mine = jnp.sum(parts, axis=0)
    mine, far = lax.optimization_barrier((mine, far))
    low = jnp.where(core == 0, far[:, :HALF], back)
    high = jnp.where(core == 0, back, far[:, :HALF])
    parts = lax.all_to_all(
        jnp.broadcast_to(mine.reshape(1, 8, 4, LANES), (4, 8, 4, LANES)).reshape(32, 4, LANES),
        AXES, 0, 0, axis_index_groups=lines_along_z(16),
    )
    last = (NX - 1) * LANES
    corner_below = shifted_by(jnp.concatenate([low[:, last:], high[:, last:]], axis=1), "px", 1)
    corner_above = shifted_by(jnp.concatenate([plane(low, 0), plane(high, 0)], axis=1), "px", -1)
    grad_input = run_input(g, weights, below, above, low, high, corner_below, corner_above)
    parts, grad_input = lax.optimization_barrier((parts, grad_input))
    mine = jnp.sum(parts, axis=0)
    parts = lax.all_to_all(jnp.broadcast_to(mine, (16, 4, LANES)), ("px", "y"), 0, 0)
    whole = parts.reshape(4, 16 * LANES)[:, : 9 * ROWS]
    total = 16 * 16 * 64 * 128
    return grad_input.reshape(1, CH, NX, NY, LANES), whole * (1.0 / math.sqrt(total))


def solution(mesh):
    fine = Mesh(mesh.devices.reshape(8, 2, 4, 4, 4), AXES)
    dp, py = ("zlo", "core"), ("y", "zhi")
    cells = P(dp, None, "px", py, None)
    return jax.shard_map(
        local, mesh=fine, in_specs=(cells, cells, P()), out_specs=(cells, P(dp, None)), check_vma=False
    )
```

```python
import math

import jax
import jax.numpy as jnp
import numpy as np
from jax import lax
from jax.experimental import pallas as pl
from jax.experimental.pallas import tpu as pltpu
from jax.sharding import Mesh, PartitionSpec as P

AXES = ("zlo", "core", "px", "y", "zhi")
LANES = 128
CH = 64
NX = 4
NY = 4
CELLS = NX * NY * LANES
F32 = jnp.float32
BF16 = jnp.bfloat16
ROWS = 3 * CH
HALF = NX * LANES
WIDE = (NX + 2) * LANES


def plane(ref, index):
    return ref[:, index * LANES : (index + 1) * LANES]


def shift_z(x, by):
    lane = lax.broadcasted_iota(jnp.int32, x.shape, 1)
    if by == 1:
        return jnp.where(lane == 0, 0.0, pltpu.roll(x, 1, 1))
    return jnp.where(lane == LANES - 1, 0.0, pltpu.roll(x, LANES - 1, 1))


def collect_z(t):
    return shift_z(t[0:CH], -1) + t[CH : 2 * CH] + shift_z(t[2 * CH : ROWS], 1)


def over_x(get, y):
    return [
        jnp.concatenate([get(x - (a - 1), y) for x in range(NX)], axis=1) for a in range(3)
    ]


def dot_nt(x, y):
    return lax.dot_general(x, y, (((1,), (1,)), ((), ())), preferred_element_type=F32)


def all_shifts(cells):
    cells = cells.astype(F32)
    return jnp.concatenate([shift_z(cells, 1), cells, shift_z(cells, -1)], axis=0).astype(BF16)


def inner_kernel(g_ref, a_ref, gk_ref, row_ref, column_ref, a3_ref):
    def get(x, y):
        if x < 0 or x >= NX:
            return jnp.zeros((CH, LANES), BF16)
        return plane(g_ref, x * NY + y)

    for y in range(NY):
        for x in range(NX):
            a3_ref[:, x * LANES : (x + 1) * LANES] = all_shifts(plane(a_ref, x * NY + y))
        if y in (0, NY - 1):
            at = y // (NY - 1) * HALF
            row_ref[:, at : at + HALF] = a3_ref[...]
        for side in range(2):
            at = side * HALF + y * LANES
            column_ref[:, at : at + LANES] = plane(a3_ref, side * (NX - 1))
        taps = [b for b in range(3) if 0 <= y - (b - 1) < NY]
        rows = []
        for b in taps:
            rows += over_x(get, y - (b - 1))
        first, last = (taps[0] * ROWS, (taps[-1] + 1) * ROWS)
        terms = dot_nt(jnp.concatenate(rows, axis=0), a3_ref[...])
        if y == 0:
            gk_ref[first:last, :] = terms
            gk_ref[last:, :] = jnp.zeros((3 * ROWS - last, ROWS), F32)
        else:
            gk_ref[first:last, :] += terms


def message_kernel(
    core_ref, g_ref, gk_ref, row_ref, column_ref, below_ref, above_ref, far_ref, msg_ref, wide_ref, rim_ref, far3_ref
):
    upward = core_ref[0] == 0

    def near(low, high):
        return jnp.where(upward, low, high)

    rim_ref[:, 0:LANES] = all_shifts(near(plane(below_ref, NY), plane(below_ref, NY + 1)))
    rim_ref[:, LANES : LANES + HALF] = near(row_ref[:, 0:HALF], row_ref[:, HALF : 2 * HALF])
    rim_ref[:, LANES + HALF : WIDE] = all_shifts(near(plane(above_ref, NY), plane(above_ref, NY + 1)))
    for x in range(NX):
        far3_ref[:, x * LANES : (x + 1) * LANES] = all_shifts(plane(far_ref, NX + x))
    own = [near(plane(below_ref, 0), plane(below_ref, NY - 1))]
    own += [near(plane(g_ref, x * NY), plane(g_ref, x * NY + NY - 1)) for x in range(NX)]
    own += [near(plane(above_ref, 0), plane(above_ref, NY - 1))]

    def across(a):
        of_far = dot_nt(far_ref[:, 0:HALF], rim_ref[:, a * LANES : a * LANES + HALF])
        of_own = dot_nt(jnp.concatenate(own[2 - a : 2 - a + NX], axis=1), far3_ref[...])
        return jnp.where(upward, of_own, of_far), jnp.where(upward, of_far, of_own)

    pairs = [across(a) for a in range(3)]

    def block(a, b):
        value = gk_ref[b * ROWS + a * CH : b * ROWS + (a + 1) * CH, :]
        if a != 1:
            face, side = (above_ref, 1) if a == 0 else (below_ref, 0)
            rows = [y for y in range(NY) if 0 <= y - (b - 1) < NY]
            of_g = (rows[0] - (b - 1)) * LANES
            of_a = side * HALF + rows[0] * LANES
            size = len(rows) * LANES
            value = value + dot_nt(face[:, of_g : of_g + size], column_ref[:, of_a : of_a + size])
        if b != 1:
            value = value + pairs[a][b // 2]
        return value

    pad = jnp.zeros((CH, 2 * LANES - ROWS), F32)
    lane = lax.broadcasted_iota(jnp.int32, (CH, LANES), 1)
    for m in range(5):
        even = jnp.concatenate([block(*divmod(2 * m, 3)), pad], axis=1)
        wide_ref[3 * m] = even[:, 0:LANES]
        if m == 4:
            wide_ref[3 * m + 1] = even[:, LANES:]
            wide_ref[3 * m + 2] = jnp.zeros((CH, LANES), F32)
            wide_ref[3 * m + 3] = jnp.zeros((CH, LANES), F32)
            break
        odd = jnp.concatenate([block(*divmod(2 * m + 1, 3)), pad], axis=1)
        odd = pltpu.roll(odd, CH, 1)
        wide_ref[3 * m + 1] = jnp.where(lane < CH, even[:, LANES:], odd[:, 0:LANES])
        wide_ref[3 * m + 2] = odd[:, LANES:]
    for s in range(8):
        for column in range(16):
            at = column % 4 * LANES
            msg_ref[s * 4 + column // 4, :, at : at + LANES] = wide_ref[
                column, pl.ds(s, 8, stride=8), :
            ]


def input_kernel(
    g_ref, w_ref, below_ref, above_ref, low_ref, high_ref, corner_below_ref, corner_above_ref, out_ref
):
    def get(x, y):
        if 0 <= y < NY:
            if x < 0:
                return plane(below_ref, y)
            if x >= NX:
                return plane(above_ref, y)
            return plane(g_ref, x * NY + y)
        side = 0 if y < 0 else 1
        if x < 0:
            return plane(corner_below_ref, side)
        if x >= NX:
            return plane(corner_above_ref, side)
        return plane((low_ref, high_ref)[side], x)

    for y in range(NY):
        rows = []
        for b in range(3):
            rows += over_x(get, y - (b - 1))
        t = jnp.dot(w_ref[...], jnp.concatenate(rows, axis=0), preferred_element_type=F32)
        for x in range(NX):
            lanes = (x * NY + y) * LANES
            out_ref[:, lanes : lanes + LANES] = collect_z(
                t[:, x * LANES : (x + 1) * LANES]
            ).astype(BF16)


def call(body, out_shape, scratch=(), cost=None, **specs):
    return pl.pallas_call(
        body,
        out_shape=out_shape,
        scratch_shapes=scratch,
        cost_estimate=cost,
        compiler_params=pltpu.CompilerParams(vmem_limit_bytes=48 * 1024 * 1024),
        **specs,
    )


def run_inner(*operands):
    shape = jax.ShapeDtypeStruct
    return call(
        inner_kernel,
        (shape((3 * ROWS, ROWS), F32), shape((ROWS, 2 * HALF), BF16), shape((ROWS, 2 * HALF), BF16)),
        [pltpu.VMEM((ROWS, HALF), BF16)],
        pl.CostEstimate(flops=20 * 10**9, transcendentals=0, bytes_accessed=2**20),
    )(*operands)


def run_message(core, *operands):
    vmem = pl.BlockSpec(memory_space=pltpu.VMEM)
    return call(
        message_kernel,
        jax.ShapeDtypeStruct((32, 8, HALF), F32),
        [
            pltpu.VMEM((16, CH, LANES), F32),
            pltpu.VMEM((ROWS, WIDE), BF16),
            pltpu.VMEM((ROWS, HALF), BF16),
        ],
        in_specs=[pl.BlockSpec(memory_space=pltpu.SMEM)] + [vmem] * len(operands),
        out_specs=vmem,
    )(core.reshape(1), *operands)


def run_input(*operands):
    return call(input_kernel, jax.ShapeDtypeStruct((CH, CELLS), BF16))(*operands)


def shifted_by(x, axis, by):
    count = lax.axis_size(axis)
    pairs = [(i, i + by) for i in range(count) if 0 <= i + by < count]
    return lax.ppermute(x, axis, pairs)


def lines_along_z(first):
    sizes = [lax.axis_size(axis) for axis in AXES]
    place = np.arange(math.prod(sizes)).reshape(sizes)
    lines = place.transpose(1, 2, 3, 4, 0).reshape(-1, sizes[4] * sizes[0])
    return np.roll(lines, -first, axis=1).tolist()


def along_y(x, by):
    count = lax.axis_size("y") * lax.axis_size("zhi")
    pairs = []
    for core, step in enumerate((by, -by)):
        pairs += [(core * count + i, core * count + i + step) for i in range(count) if 0 <= i + step < count]
    return lax.ppermute(x, ("core", "y", "zhi"), pairs)


def local(activations, grad_out, kernel):
    core = lax.axis_index("core")
    g = grad_out.reshape(CH, CELLS)
    a = activations.reshape(CH, CELLS)

    def rows(cells, y):
        return jnp.concatenate([plane(cells, x * NY + y) for x in range(NX)], axis=1)

    g_low, g_high = rows(g, 0), rows(g, NY - 1)
    ahead = jnp.where(core == 0, g_high, g_low)
    ahead = jnp.concatenate([ahead, jnp.where(core == 0, rows(a, NY - 1), rows(a, 0))], axis=1)
    far = along_y(ahead, 1)
    back = along_y(jnp.where(core == 0, g_low, g_high), -1)


    weights = kernel.reshape(CH, 3, 3, ROWS).transpose(3, 2, 1, 0).reshape(ROWS, 3 * ROWS)

    def x_face(x):
        cells = g[:, x * NY * LANES : (x + 1) * NY * LANES]
        return jnp.concatenate([cells, plane(a, x * NY), plane(a, x * NY + NY - 1), cells[:, LANES:]], axis=1)

    below = shifted_by(x_face(NX - 1), "px", 1)
    above = shifted_by(x_face(0), "px", -1)
    inner = run_inner(g, a)
    weights, *inner = lax.optimization_barrier((weights, *inner))
    message = run_message(core, g, *inner, below, above, far)

    parts = lax.all_to_all(message, ("core", "px", "y"), 0, 0)
    mine = jnp.sum(parts, axis=0)
    mine, far = lax.optimization_barrier((mine, far))
    low = jnp.where(core == 0, far[:, :HALF], back)
    high = jnp.where(core == 0, back, far[:, :HALF])
    parts = lax.all_to_all(
        jnp.broadcast_to(mine.reshape(1, 8, 4, LANES), (4, 8, 4, LANES)).reshape(32, 4, LANES),
        AXES, 0, 0, axis_index_groups=lines_along_z(8),
    )
    last = (NX - 1) * LANES
    corner_below = shifted_by(jnp.concatenate([low[:, last:], high[:, last:]], axis=1), "px", 1)
    corner_above = shifted_by(jnp.concatenate([plane(low, 0), plane(high, 0)], axis=1), "px", -1)
    grad_input = run_input(g, weights, below, above, low, high, corner_below, corner_above)
    parts, grad_input = lax.optimization_barrier((parts, grad_input))
    mine = jnp.sum(parts, axis=0)
    parts = lax.all_to_all(jnp.broadcast_to(mine, (16, 4, LANES)), ("px", "y"), 0, 0)
    whole = parts.reshape(4, 16 * LANES)[:, : 9 * ROWS]
    total = 16 * 16 * 64 * 128
    return grad_input.reshape(1, CH, NX, NY, LANES), whole * (1.0 / math.sqrt(total))


def solution(mesh):
    fine = Mesh(mesh.devices.reshape(8, 2, 4, 4, 4), AXES)
    dp, py = ("zlo", "core"), ("y", "zhi")
    cells = P(dp, None, "px", py, None)
    return jax.shard_map(
        local, mesh=fine, in_specs=(cells, cells, P()), out_specs=(cells, P(dp, None)), check_vma=False
    )
```

```python
import math

import jax
import jax.numpy as jnp
import numpy as np
from jax import lax
from jax.experimental import pallas as pl
from jax.experimental.pallas import tpu as pltpu
from jax.sharding import Mesh, PartitionSpec as P

AXES = ("zlo", "core", "px", "y", "zhi")
LANES = 128
CH = 64
NX = 4
NY = 4
CELLS = NX * NY * LANES
F32 = jnp.float32
BF16 = jnp.bfloat16
ROWS = 3 * CH
HALF = NX * LANES
WIDE = (NX + 2) * LANES


def plane(ref, index):
    return ref[:, index * LANES : (index + 1) * LANES]


def shift_z(x, by):
    lane = lax.broadcasted_iota(jnp.int32, x.shape, 1)
    if by == 1:
        return jnp.where(lane == 0, 0.0, pltpu.roll(x, 1, 1))
    return jnp.where(lane == LANES - 1, 0.0, pltpu.roll(x, LANES - 1, 1))


def collect_z(t):
    return shift_z(t[0:CH], -1) + t[CH : 2 * CH] + shift_z(t[2 * CH : ROWS], 1)


def over_x(get, y):
    return [
        jnp.concatenate([get(x - (a - 1), y) for x in range(NX)], axis=1) for a in range(3)
    ]


def dot_nt(x, y):
    return lax.dot_general(x, y, (((1,), (1,)), ((), ())), preferred_element_type=F32)


def all_shifts(cells):
    cells = cells.astype(F32)
    return jnp.concatenate([shift_z(cells, 1), cells, shift_z(cells, -1)], axis=0).astype(BF16)


def inner_kernel(g_ref, a_ref, gk_ref, row_ref, column_ref, a3_ref):
    def get(x, y):
        if x < 0 or x >= NX:
            return jnp.zeros((CH, LANES), BF16)
        return plane(g_ref, x * NY + y)

    for y in range(NY):
        for x in range(NX):
            a3_ref[:, x * LANES : (x + 1) * LANES] = all_shifts(plane(a_ref, x * NY + y))
        if y in (0, NY - 1):
            at = y // (NY - 1) * HALF
            row_ref[:, at : at + HALF] = a3_ref[...]
        for side in range(2):
            at = side * HALF + y * LANES
            column_ref[:, at : at + LANES] = plane(a3_ref, side * (NX - 1))
        taps = [b for b in range(3) if 0 <= y - (b - 1) < NY]
        rows = []
        for b in taps:
            rows += over_x(get, y - (b - 1))
        first, last = (taps[0] * ROWS, (taps[-1] + 1) * ROWS)
        terms = dot_nt(jnp.concatenate(rows, axis=0), a3_ref[...])
        if y == 0:
            gk_ref[first:last, :] = terms
            gk_ref[last:, :] = jnp.zeros((3 * ROWS - last, ROWS), F32)
        else:
            gk_ref[first:last, :] += terms


def message_kernel(
    core_ref, g_ref, gk_ref, row_ref, column_ref, below_ref, above_ref, far_ref, msg_ref, wide_ref, rim_ref, far3_ref
):
    upward = core_ref[0] == 0

    def near(low, high):
        return jnp.where(upward, low, high)

    rim_ref[:, 0:LANES] = all_shifts(near(plane(below_ref, NY), plane(below_ref, NY + 1)))
    rim_ref[:, LANES : LANES + HALF] = near(row_ref[:, 0:HALF], row_ref[:, HALF : 2 * HALF])
    rim_ref[:, LANES + HALF : WIDE] = all_shifts(near(plane(above_ref, NY), plane(above_ref, NY + 1)))
    for x in range(NX):
        far3_ref[:, x * LANES : (x + 1) * LANES] = all_shifts(plane(far_ref, NX + x))
    own = [near(plane(below_ref, 0), plane(below_ref, NY - 1))]
    own += [near(plane(g_ref, x * NY), plane(g_ref, x * NY + NY - 1)) for x in range(NX)]
    own += [near(plane(above_ref, 0), plane(above_ref, NY - 1))]

    def across(a):
        of_far = dot_nt(far_ref[:, 0:HALF], rim_ref[:, a * LANES : a * LANES + HALF])
        of_own = dot_nt(jnp.concatenate(own[2 - a : 2 - a + NX], axis=1), far3_ref[...])
        return jnp.where(upward, of_own, of_far), jnp.where(upward, of_far, of_own)

    pairs = [across(a) for a in range(3)]

    def block(a, b):
        value = gk_ref[b * ROWS + a * CH : b * ROWS + (a + 1) * CH, :]
        if a != 1:
            face, side = (above_ref, 1) if a == 0 else (below_ref, 0)
            rows = [y for y in range(NY) if 0 <= y - (b - 1) < NY]
            of_g = (rows[0] - (b - 1)) * LANES
            of_a = side * HALF + rows[0] * LANES
            size = len(rows) * LANES
            value = value + dot_nt(face[:, of_g : of_g + size], column_ref[:, of_a : of_a + size])
        if b != 1:
            value = value + pairs[a][b // 2]
        return value

    pad = jnp.zeros((CH, 2 * LANES - ROWS), F32)
    lane = lax.broadcasted_iota(jnp.int32, (CH, LANES), 1)
    for m in range(5):
        even = jnp.concatenate([block(*divmod(2 * m, 3)), pad], axis=1)
        wide_ref[3 * m] = even[:, 0:LANES]
        if m == 4:
            wide_ref[3 * m + 1] = even[:, LANES:]
            wide_ref[3 * m + 2] = jnp.zeros((CH, LANES), F32)
            wide_ref[3 * m + 3] = jnp.zeros((CH, LANES), F32)
            break
        odd = jnp.concatenate([block(*divmod(2 * m + 1, 3)), pad], axis=1)
        odd = pltpu.roll(odd, CH, 1)
        wide_ref[3 * m + 1] = jnp.where(lane < CH, even[:, LANES:], odd[:, 0:LANES])
        wide_ref[3 * m + 2] = odd[:, LANES:]
    for s in range(8):
        for column in range(16):
            at = column % 4 * LANES
            msg_ref[s * 4 + column // 4, :, at : at + LANES] = wide_ref[
                column, pl.ds(s, 8, stride=8), :
            ]


def input_kernel(
    g_ref, w_ref, below_ref, above_ref, low_ref, high_ref, corner_below_ref, corner_above_ref, out_ref
):
    def get(x, y):
        if 0 <= y < NY:
            if x < 0:
                return plane(below_ref, y)
            if x >= NX:
                return plane(above_ref, y)
            return plane(g_ref, x * NY + y)
        side = 0 if y < 0 else 1
        if x < 0:
            return plane(corner_below_ref, side)
        if x >= NX:
            return plane(corner_above_ref, side)
        return plane((low_ref, high_ref)[side], x)

    for y in range(NY):
        rows = []
        for b in range(3):
            rows += over_x(get, y - (b - 1))
        t = jnp.dot(w_ref[...], jnp.concatenate(rows, axis=0), preferred_element_type=F32)
        for x in range(NX):
            lanes = (x * NY + y) * LANES
            out_ref[:, lanes : lanes + LANES] = collect_z(
                t[:, x * LANES : (x + 1) * LANES]
            ).astype(BF16)


def call(body, out_shape, scratch=(), cost=None, **specs):
    return pl.pallas_call(
        body,
        out_shape=out_shape,
        scratch_shapes=scratch,
        cost_estimate=cost,
        compiler_params=pltpu.CompilerParams(vmem_limit_bytes=48 * 1024 * 1024),
        **specs,
    )


def run_inner(*operands):
    shape = jax.ShapeDtypeStruct
    return call(
        inner_kernel,
        (shape((3 * ROWS, ROWS), F32), shape((ROWS, 2 * HALF), BF16), shape((ROWS, 2 * HALF), BF16)),
        [pltpu.VMEM((ROWS, HALF), BF16)],
        pl.CostEstimate(flops=20 * 10**9, transcendentals=0, bytes_accessed=2**20),
    )(*operands)


def run_message(core, *operands):
    vmem = pl.BlockSpec(memory_space=pltpu.VMEM)
    return call(
        message_kernel,
        jax.ShapeDtypeStruct((32, 8, HALF), F32),
        [
            pltpu.VMEM((16, CH, LANES), F32),
            pltpu.VMEM((ROWS, WIDE), BF16),
            pltpu.VMEM((ROWS, HALF), BF16),
        ],
        in_specs=[pl.BlockSpec(memory_space=pltpu.SMEM)] + [vmem] * len(operands),
        out_specs=vmem,
    )(core.reshape(1), *operands)


def run_input(*operands):
    return call(input_kernel, jax.ShapeDtypeStruct((CH, CELLS), BF16))(*operands)


def shifted_by(x, axis, by):
    count = lax.axis_size(axis)
    pairs = [(i, i + by) for i in range(count) if 0 <= i + by < count]
    return lax.ppermute(x, axis, pairs)


def lines_along_z(first):
    sizes = [lax.axis_size(axis) for axis in AXES]
    place = np.arange(math.prod(sizes)).reshape(sizes)
    lines = place.transpose(1, 2, 3, 4, 0).reshape(-1, sizes[4] * sizes[0])
    return np.roll(lines, -first, axis=1).tolist()


def along_y(x, by):
    count = lax.axis_size("y") * lax.axis_size("zhi")
    pairs = []
    for core, step in enumerate((by, -by)):
        pairs += [(core * count + i, core * count + i + step) for i in range(count) if 0 <= i + step < count]
    return lax.ppermute(x, ("core", "y", "zhi"), pairs)


def local(activations, grad_out, kernel):
    core = lax.axis_index("core")
    g = grad_out.reshape(CH, CELLS)
    a = activations.reshape(CH, CELLS)

    def rows(cells, y):
        return jnp.concatenate([plane(cells, x * NY + y) for x in range(NX)], axis=1)

    g_low, g_high = rows(g, 0), rows(g, NY - 1)
    ahead = jnp.where(core == 0, g_high, g_low)
    ahead = jnp.concatenate([ahead, jnp.where(core == 0, rows(a, NY - 1), rows(a, 0))], axis=1)
    far = along_y(ahead, 1)
    back = along_y(jnp.where(core == 0, g_low, g_high), -1)


    weights = kernel.reshape(CH, 3, 3, ROWS).transpose(3, 2, 1, 0).reshape(ROWS, 3 * ROWS)

    def x_face(x):
        cells = g[:, x * NY * LANES : (x + 1) * NY * LANES]
        return jnp.concatenate([cells, plane(a, x * NY), plane(a, x * NY + NY - 1), cells[:, LANES:]], axis=1)

    below = shifted_by(x_face(NX - 1), "px", 1)
    above = shifted_by(x_face(0), "px", -1)
    inner = run_inner(g, a)
    weights, *inner = lax.optimization_barrier((weights, *inner))
    message = run_message(core, g, *inner, below, above, far)

    parts = lax.all_to_all(message, ("core", "px", "y"), 0, 0)
    mine = jnp.sum(parts, axis=0)
    mine, far = lax.optimization_barrier((mine, far))
    low = jnp.where(core == 0, far[:, :HALF], back)
    high = jnp.where(core == 0, back, far[:, :HALF])
    parts = lax.all_to_all(
        jnp.broadcast_to(mine.reshape(1, 8, 4, LANES), (4, 8, 4, LANES)).reshape(32, 4, LANES),
        AXES, 0, 0, axis_index_groups=lines_along_z(24),
    )
    last = (NX - 1) * LANES
    corner_below = shifted_by(jnp.concatenate([low[:, last:], high[:, last:]], axis=1), "px", 1)
    corner_above = shifted_by(jnp.concatenate([plane(low, 0), plane(high, 0)], axis=1), "px", -1)
    grad_input = run_input(g, weights, below, above, low, high, corner_below, corner_above)
    parts, grad_input = lax.optimization_barrier((parts, grad_input))
    mine = jnp.sum(parts, axis=0)
    parts = lax.all_to_all(jnp.broadcast_to(mine, (16, 4, LANES)), ("px", "y"), 0, 0)
    whole = parts.reshape(4, 16 * LANES)[:, : 9 * ROWS]
    total = 16 * 16 * 64 * 128
    return grad_input.reshape(1, CH, NX, NY, LANES), whole * (1.0 / math.sqrt(total))


def solution(mesh):
    fine = Mesh(mesh.devices.reshape(8, 2, 4, 4, 4), AXES)
    dp, py = ("zlo", "core"), ("y", "zhi")
    cells = P(dp, None, "px", py, None)
    return jax.shard_map(
        local, mesh=fine, in_specs=(cells, cells, P()), out_specs=(cells, P(dp, None)), check_vma=False
    )
```

```python
import math

import jax
import jax.numpy as jnp
import numpy as np
from jax import lax
from jax.experimental import pallas as pl
from jax.experimental.pallas import tpu as pltpu
from jax.sharding import Mesh, PartitionSpec as P

AXES = ("zlo", "core", "px", "y", "zhi")
LANES = 128
CH = 64
NX = 4
NY = 4
CELLS = NX * NY * LANES
F32 = jnp.float32
BF16 = jnp.bfloat16
ROWS = 3 * CH
HALF = NX * LANES
WIDE = (NX + 2) * LANES


def plane(ref, index):
    return ref[:, index * LANES : (index + 1) * LANES]


def shift_z(x, by):
    lane = lax.broadcasted_iota(jnp.int32, x.shape, 1)
    if by == 1:
        return jnp.where(lane == 0, 0.0, pltpu.roll(x, 1, 1))
    return jnp.where(lane == LANES - 1, 0.0, pltpu.roll(x, LANES - 1, 1))


def collect_z(t):
    return shift_z(t[0:CH], -1) + t[CH : 2 * CH] + shift_z(t[2 * CH : ROWS], 1)


def over_x(get, y):
    return [
        jnp.concatenate([get(x - (a - 1), y) for x in range(NX)], axis=1) for a in range(3)
    ]


def dot_nt(x, y):
    return lax.dot_general(x, y, (((1,), (1,)), ((), ())), preferred_element_type=F32)


def all_shifts(cells):
    cells = cells.astype(F32)
    return jnp.concatenate([shift_z(cells, 1), cells, shift_z(cells, -1)], axis=0).astype(BF16)


def inner_kernel(g_ref, a_ref, gk_ref, row_ref, column_ref, a3_ref):
    def get(x, y):
        if x < 0 or x >= NX:
            return jnp.zeros((CH, LANES), BF16)
        return plane(g_ref, x * NY + y)

    for y in range(NY):
        for x in range(NX):
            a3_ref[:, x * LANES : (x + 1) * LANES] = all_shifts(plane(a_ref, x * NY + y))
        if y in (0, NY - 1):
            at = y // (NY - 1) * HALF
            row_ref[:, at : at + HALF] = a3_ref[...]
        for side in range(2):
            at = side * HALF + y * LANES
            column_ref[:, at : at + LANES] = plane(a3_ref, side * (NX - 1))
        taps = [b for b in range(3) if 0 <= y - (b - 1) < NY]
        rows = []
        for b in taps:
            rows += over_x(get, y - (b - 1))
        first, last = (taps[0] * ROWS, (taps[-1] + 1) * ROWS)
        terms = dot_nt(jnp.concatenate(rows, axis=0), a3_ref[...])
        if y == 0:
            gk_ref[first:last, :] = terms
            gk_ref[last:, :] = jnp.zeros((3 * ROWS - last, ROWS), F32)
        else:
            gk_ref[first:last, :] += terms


def message_kernel(
    core_ref, g_ref, gk_ref, row_ref, column_ref, below_ref, above_ref, far_ref, msg_ref, wide_ref, rim_ref, far3_ref
):
    upward = core_ref[0] == 0

    def near(low, high):
        return jnp.where(upward, low, high)

    rim_ref[:, 0:LANES] = all_shifts(near(plane(below_ref, NY), plane(below_ref, NY + 1)))
    rim_ref[:, LANES : LANES + HALF] = near(row_ref[:, 0:HALF], row_ref[:, HALF : 2 * HALF])
    rim_ref[:, LANES + HALF : WIDE] = all_shifts(near(plane(above_ref, NY), plane(above_ref, NY + 1)))
    for x in range(NX):
        far3_ref[:, x * LANES : (x + 1) * LANES] = all_shifts(plane(far_ref, NX + x))
    own = [near(plane(below_ref, 0), plane(below_ref, NY - 1))]
    own += [near(plane(g_ref, x * NY), plane(g_ref, x * NY + NY - 1)) for x in range(NX)]
    own += [near(plane(above_ref, 0), plane(above_ref, NY - 1))]

    def across(a):
        of_far = dot_nt(far_ref[:, 0:HALF], rim_ref[:, a * LANES : a * LANES + HALF])
        of_own = dot_nt(jnp.concatenate(own[2 - a : 2 - a + NX], axis=1), far3_ref[...])
        return jnp.where(upward, of_own, of_far), jnp.where(upward, of_far, of_own)

    pairs = [across(a) for a in range(3)]

    def block(a, b):
        value = gk_ref[b * ROWS + a * CH : b * ROWS + (a + 1) * CH, :]
        if a != 1:
            face, side = (above_ref, 1) if a == 0 else (below_ref, 0)
            rows = [y for y in range(NY) if 0 <= y - (b - 1) < NY]
            of_g = (rows[0] - (b - 1)) * LANES
            of_a = side * HALF + rows[0] * LANES
            size = len(rows) * LANES
            value = value + dot_nt(face[:, of_g : of_g + size], column_ref[:, of_a : of_a + size])
        if b != 1:
            value = value + pairs[a][b // 2]
        return value

    pad = jnp.zeros((CH, 2 * LANES - ROWS), F32)
    lane = lax.broadcasted_iota(jnp.int32, (CH, LANES), 1)
    for m in range(5):
        even = jnp.concatenate([block(*divmod(2 * m, 3)), pad], axis=1)
        wide_ref[3 * m] = even[:, 0:LANES]
        if m == 4:
            wide_ref[3 * m + 1] = even[:, LANES:]
            wide_ref[3 * m + 2] = jnp.zeros((CH, LANES), F32)
            wide_ref[3 * m + 3] = jnp.zeros((CH, LANES), F32)
            break
        odd = jnp.concatenate([block(*divmod(2 * m + 1, 3)), pad], axis=1)
        odd = pltpu.roll(odd, CH, 1)
        wide_ref[3 * m + 1] = jnp.where(lane < CH, even[:, LANES:], odd[:, 0:LANES])
        wide_ref[3 * m + 2] = odd[:, LANES:]
    for s in range(8):
        for column in range(16):
            at = column % 4 * LANES
            msg_ref[s * 4 + column // 4, :, at : at + LANES] = wide_ref[
                column, pl.ds(s, 8, stride=8), :
            ]


def input_kernel(
    g_ref, w_ref, below_ref, above_ref, low_ref, high_ref, corner_below_ref, corner_above_ref, out_ref
):
    def get(x, y):
        if 0 <= y < NY:
            if x < 0:
                return plane(below_ref, y)
            if x >= NX:
                return plane(above_ref, y)
            return plane(g_ref, x * NY + y)
        side = 0 if y < 0 else 1
        if x < 0:
            return plane(corner_below_ref, side)
        if x >= NX:
            return plane(corner_above_ref, side)
        return plane((low_ref, high_ref)[side], x)

    for y in range(NY):
        rows = []
        for b in range(3):
            rows += over_x(get, y - (b - 1))
        t = jnp.dot(w_ref[...], jnp.concatenate(rows, axis=0), preferred_element_type=F32)
        for x in range(NX):
            lanes = (x * NY + y) * LANES
            out_ref[:, lanes : lanes + LANES] = collect_z(
                t[:, x * LANES : (x + 1) * LANES]
            ).astype(BF16)


def call(body, out_shape, scratch=(), cost=None, **specs):
    return pl.pallas_call(
        body,
        out_shape=out_shape,
        scratch_shapes=scratch,
        cost_estimate=cost,
        compiler_params=pltpu.CompilerParams(vmem_limit_bytes=48 * 1024 * 1024),
        **specs,
    )


def run_inner(*operands):
    shape = jax.ShapeDtypeStruct
    return call(
        inner_kernel,
        (shape((3 * ROWS, ROWS), F32), shape((ROWS, 2 * HALF), BF16), shape((ROWS, 2 * HALF), BF16)),
        [pltpu.VMEM((ROWS, HALF), BF16)],
        pl.CostEstimate(flops=20 * 10**9, transcendentals=0, bytes_accessed=2**20),
    )(*operands)


def run_message(core, *operands):
    vmem = pl.BlockSpec(memory_space=pltpu.VMEM)
    return call(
        message_kernel,
        jax.ShapeDtypeStruct((32, 8, HALF), F32),
        [
            pltpu.VMEM((16, CH, LANES), F32),
            pltpu.VMEM((ROWS, WIDE), BF16),
            pltpu.VMEM((ROWS, HALF), BF16),
        ],
        in_specs=[pl.BlockSpec(memory_space=pltpu.SMEM)] + [vmem] * len(operands),
        out_specs=vmem,
    )(core.reshape(1), *operands)


def run_input(*operands):
    return call(input_kernel, jax.ShapeDtypeStruct((CH, CELLS), BF16))(*operands)


def shifted_by(x, axis, by):
    count = lax.axis_size(axis)
    pairs = [(i, i + by) for i in range(count) if 0 <= i + by < count]
    return lax.ppermute(x, axis, pairs)


def lines_along_z(first):
    sizes = [lax.axis_size(axis) for axis in AXES]
    place = np.arange(math.prod(sizes)).reshape(sizes)
    lines = place.transpose(1, 2, 3, 4, 0).reshape(-1, sizes[4] * sizes[0])
    return np.roll(lines, -first, axis=1).tolist()


def along_y(x, by):
    count = lax.axis_size("y") * lax.axis_size("zhi")
    pairs = []
    for core, step in enumerate((by, -by)):
        pairs += [(core * count + i, core * count + i + step) for i in range(count) if 0 <= i + step < count]
    return lax.ppermute(x, ("core", "y", "zhi"), pairs)


def local(activations, grad_out, kernel):
    core = lax.axis_index("core")
    g = grad_out.reshape(CH, CELLS)
    a = activations.reshape(CH, CELLS)

    def rows(cells, y):
        return jnp.concatenate([plane(cells, x * NY + y) for x in range(NX)], axis=1)

    g_low, g_high = rows(g, 0), rows(g, NY - 1)
    ahead = jnp.where(core == 0, g_high, g_low)
    ahead = jnp.concatenate([ahead, jnp.where(core == 0, rows(a, NY - 1), rows(a, 0))], axis=1)
    far = along_y(ahead, 1)
    back = along_y(jnp.where(core == 0, g_low, g_high), -1)


    weights = kernel.reshape(CH, 3, 3, ROWS).transpose(3, 2, 1, 0).reshape(ROWS, 3 * ROWS)

    def x_face(x):
        cells = g[:, x * NY * LANES : (x + 1) * NY * LANES]
        return jnp.concatenate([cells, plane(a, x * NY), plane(a, x * NY + NY - 1), cells[:, LANES:]], axis=1)

    below = shifted_by(x_face(NX - 1), "px", 1)
    above = shifted_by(x_face(0), "px", -1)
    inner = run_inner(g, a)
    weights, *inner = lax.optimization_barrier((weights, *inner))
    message = run_message(core, g, *inner, below, above, far)

    parts = lax.all_to_all(message, ("core", "px", "y"), 0, 0)
    mine = jnp.sum(parts, axis=0)
    mine, far = lax.optimization_barrier((mine, far))
    low = jnp.where(core == 0, far[:, :HALF], back)
    high = jnp.where(core == 0, back, far[:, :HALF])
    parts = lax.all_to_all(
        jnp.broadcast_to(mine.reshape(1, 8, 4, LANES), (4, 8, 4, LANES)).reshape(32, 4, LANES),
        AXES, 0, 0, axis_index_groups=lines_along_z(16),
    )
    last = (NX - 1) * LANES
    corner_below = shifted_by(jnp.concatenate([low[:, last:], high[:, last:]], axis=1), "px", 1)
    corner_above = shifted_by(jnp.concatenate([plane(low, 0), plane(high, 0)], axis=1), "px", -1)
    mine = jnp.sum(parts, axis=0)
    mine, g = lax.optimization_barrier((mine, g))
    grad_input = run_input(g, weights, below, above, low, high, corner_below, corner_above)
    parts = lax.all_to_all(jnp.broadcast_to(mine, (16, 4, LANES)), ("px", "y"), 0, 0)
    whole = parts.reshape(4, 16 * LANES)[:, : 9 * ROWS]
    total = 16 * 16 * 64 * 128
    return grad_input.reshape(1, CH, NX, NY, LANES), whole * (1.0 / math.sqrt(total))


def solution(mesh):
    fine = Mesh(mesh.devices.reshape(8, 2, 4, 4, 4), AXES)
    dp, py = ("zlo", "core"), ("y", "zhi")
    cells = P(dp, None, "px", py, None)
    return jax.shard_map(
        local, mesh=fine, in_specs=(cells, cells, P()), out_specs=(cells, P(dp, None)), check_vma=False
    )
```

```python
import math

import jax
import jax.numpy as jnp
import numpy as np
from jax import lax
from jax.experimental import pallas as pl
from jax.experimental.pallas import tpu as pltpu
from jax.sharding import Mesh, PartitionSpec as P

AXES = ("zlo", "core", "px", "y", "zhi")
LANES = 128
CH = 64
NX = 4
NY = 4
CELLS = NX * NY * LANES
F32 = jnp.float32
BF16 = jnp.bfloat16
ROWS = 3 * CH
HALF = NX * LANES
WIDE = (NX + 2) * LANES


def plane(ref, index):
    return ref[:, index * LANES : (index + 1) * LANES]


def shift_z(x, by):
    lane = lax.broadcasted_iota(jnp.int32, x.shape, 1)
    if by == 1:
        return jnp.where(lane == 0, 0.0, pltpu.roll(x, 1, 1))
    return jnp.where(lane == LANES - 1, 0.0, pltpu.roll(x, LANES - 1, 1))


def collect_z(t):
    return shift_z(t[0:CH], -1) + t[CH : 2 * CH] + shift_z(t[2 * CH : ROWS], 1)


def over_x(get, y):
    return [
        jnp.concatenate([get(x - (a - 1), y) for x in range(NX)], axis=1) for a in range(3)
    ]


def dot_nt(x, y):
    return lax.dot_general(x, y, (((1,), (1,)), ((), ())), preferred_element_type=F32)


def all_shifts(cells):
    cells = cells.astype(F32)
    return jnp.concatenate([shift_z(cells, 1), cells, shift_z(cells, -1)], axis=0).astype(BF16)


def inner_kernel(g_ref, a_ref, gk_ref, row_ref, column_ref, a3_ref):
    def get(x, y):
        if x < 0 or x >= NX:
            return jnp.zeros((CH, LANES), BF16)
        return plane(g_ref, x * NY + y)

    for y in range(NY):
        for x in range(NX):
            a3_ref[:, x * LANES : (x + 1) * LANES] = all_shifts(plane(a_ref, x * NY + y))
        if y in (0, NY - 1):
            at = y // (NY - 1) * HALF
            row_ref[:, at : at + HALF] = a3_ref[...]
        for side in range(2):
            at = side * HALF + y * LANES
            column_ref[:, at : at + LANES] = plane(a3_ref, side * (NX - 1))
        taps = [b for b in range(3) if 0 <= y - (b - 1) < NY]
        rows = []
        for b in taps:
            rows += over_x(get, y - (b - 1))
        first, last = (taps[0] * ROWS, (taps[-1] + 1) * ROWS)
        terms = dot_nt(jnp.concatenate(rows, axis=0), a3_ref[...])
        if y == 0:
            gk_ref[first:last, :] = terms
            gk_ref[last:, :] = jnp.zeros((3 * ROWS - last, ROWS), F32)
        else:
            gk_ref[first:last, :] += terms


def message_kernel(
    core_ref, g_ref, gk_ref, row_ref, column_ref, below_ref, above_ref, far_ref, msg_ref, wide_ref, rim_ref, far3_ref
):
    upward = core_ref[0] == 0

    def near(low, high):
        return jnp.where(upward, low, high)

    rim_ref[:, 0:LANES] = all_shifts(near(plane(below_ref, NY), plane(below_ref, NY + 1)))
    rim_ref[:, LANES : LANES + HALF] = near(row_ref[:, 0:HALF], row_ref[:, HALF : 2 * HALF])
    rim_ref[:, LANES + HALF : WIDE] = all_shifts(near(plane(above_ref, NY), plane(above_ref, NY + 1)))
    for x in range(NX):
        far3_ref[:, x * LANES : (x + 1) * LANES] = all_shifts(plane(far_ref, NX + x))
    own = [near(plane(below_ref, 0), plane(below_ref, NY - 1))]
    own += [near(plane(g_ref, x * NY), plane(g_ref, x * NY + NY - 1)) for x in range(NX)]
    own += [near(plane(above_ref, 0), plane(above_ref, NY - 1))]

    def across(a):
        of_far = dot_nt(far_ref[:, 0:HALF], rim_ref[:, a * LANES : a * LANES + HALF])
        of_own = dot_nt(jnp.concatenate(own[2 - a : 2 - a + NX], axis=1), far3_ref[...])
        return jnp.where(upward, of_own, of_far), jnp.where(upward, of_far, of_own)

    pairs = [across(a) for a in range(3)]

    def block(a, b):
        value = gk_ref[b * ROWS + a * CH : b * ROWS + (a + 1) * CH, :]
        if a != 1:
            face, side = (above_ref, 1) if a == 0 else (below_ref, 0)
            rows = [y for y in range(NY) if 0 <= y - (b - 1) < NY]
            of_g = (rows[0] - (b - 1)) * LANES
            of_a = side * HALF + rows[0] * LANES
            size = len(rows) * LANES
            value = value + dot_nt(face[:, of_g : of_g + size], column_ref[:, of_a : of_a + size])
        if b != 1:
            value = value + pairs[a][b // 2]
        return value

    pad = jnp.zeros((CH, 2 * LANES - ROWS), F32)
    lane = lax.broadcasted_iota(jnp.int32, (CH, LANES), 1)
    for m in range(5):
        even = jnp.concatenate([block(*divmod(2 * m, 3)), pad], axis=1)
        wide_ref[3 * m] = even[:, 0:LANES]
        if m == 4:
            wide_ref[3 * m + 1] = even[:, LANES:]
            wide_ref[3 * m + 2] = jnp.zeros((CH, LANES), F32)
            wide_ref[3 * m + 3] = jnp.zeros((CH, LANES), F32)
            break
        odd = jnp.concatenate([block(*divmod(2 * m + 1, 3)), pad], axis=1)
        odd = pltpu.roll(odd, CH, 1)
        wide_ref[3 * m + 1] = jnp.where(lane < CH, even[:, LANES:], odd[:, 0:LANES])
        wide_ref[3 * m + 2] = odd[:, LANES:]
    for s in range(8):
        for column in range(16):
            at = column % 4 * LANES
            msg_ref[s * 4 + column // 4, :, at : at + LANES] = wide_ref[
                column, pl.ds(s, 8, stride=8), :
            ]


def input_kernel(
    g_ref, w_ref, below_ref, above_ref, low_ref, high_ref, corner_below_ref, corner_above_ref, out_ref
):
    def get(x, y):
        if 0 <= y < NY:
            if x < 0:
                return plane(below_ref, y)
            if x >= NX:
                return plane(above_ref, y)
            return plane(g_ref, x * NY + y)
        side = 0 if y < 0 else 1
        if x < 0:
            return plane(corner_below_ref, side)
        if x >= NX:
            return plane(corner_above_ref, side)
        return plane((low_ref, high_ref)[side], x)

    for y in range(NY):
        rows = []
        for b in range(3):
            rows += over_x(get, y - (b - 1))
        t = jnp.dot(w_ref[...], jnp.concatenate(rows, axis=0), preferred_element_type=F32)
        for x in range(NX):
            lanes = (x * NY + y) * LANES
            out_ref[:, lanes : lanes + LANES] = collect_z(
                t[:, x * LANES : (x + 1) * LANES]
            ).astype(BF16)


def call(body, out_shape, scratch=(), cost=None, **specs):
    return pl.pallas_call(
        body,
        out_shape=out_shape,
        scratch_shapes=scratch,
        cost_estimate=cost,
        compiler_params=pltpu.CompilerParams(vmem_limit_bytes=48 * 1024 * 1024),
        **specs,
    )


def run_inner(*operands):
    shape = jax.ShapeDtypeStruct
    return call(
        inner_kernel,
        (shape((3 * ROWS, ROWS), F32), shape((ROWS, 2 * HALF), BF16), shape((ROWS, 2 * HALF), BF16)),
        [pltpu.VMEM((ROWS, HALF), BF16)],
        pl.CostEstimate(flops=20 * 10**9, transcendentals=0, bytes_accessed=2**20),
    )(*operands)


def run_message(core, *operands):
    vmem = pl.BlockSpec(memory_space=pltpu.VMEM)
    return call(
        message_kernel,
        jax.ShapeDtypeStruct((32, 8, HALF), F32),
        [
            pltpu.VMEM((16, CH, LANES), F32),
            pltpu.VMEM((ROWS, WIDE), BF16),
            pltpu.VMEM((ROWS, HALF), BF16),
        ],
        in_specs=[pl.BlockSpec(memory_space=pltpu.SMEM)] + [vmem] * len(operands),
        out_specs=vmem,
    )(core.reshape(1), *operands)


def rows_kernel(core_ref, g_ref, a_ref, ahead_ref, behind_ref, last_ref, first_ref):
    upward = core_ref[0] == 0
    for x in range(NX):
        low, high = (x * NY, x * NY + NY - 1)
        lanes = slice(x * LANES, (x + 1) * LANES)
        ahead_ref[:, lanes] = jnp.where(upward, plane(g_ref, high), plane(g_ref, low))
        behind_ref[:, lanes] = jnp.where(upward, plane(g_ref, low), plane(g_ref, high))
        lanes = slice(HALF + x * LANES, HALF + (x + 1) * LANES)
        ahead_ref[:, lanes] = jnp.where(upward, plane(a_ref, high), plane(a_ref, low))
    size = NY * LANES
    for x, out_ref in ((NX - 1, last_ref), (0, first_ref)):
        out_ref[:, 0:size] = g_ref[:, x * size : (x + 1) * size]
        out_ref[:, size : size + LANES] = plane(a_ref, x * NY)
        out_ref[:, size + LANES : size + 2 * LANES] = plane(a_ref, x * NY + NY - 1)


def run_rows(core, *operands):
    vmem = pl.BlockSpec(memory_space=pltpu.VMEM)
    return call(
        rows_kernel,
        tuple(jax.ShapeDtypeStruct((CH, n * LANES), BF16) for n in (2 * NX, NX, 6, 6)),
        in_specs=[pl.BlockSpec(memory_space=pltpu.SMEM), vmem, vmem],
        out_specs=(vmem,) * 4,
    )(core.reshape(1), *operands)


def run_input(*operands):
    return call(input_kernel, jax.ShapeDtypeStruct((CH, CELLS), BF16))(*operands)


def shifted_by(x, axis, by):
    count = lax.axis_size(axis)
    pairs = [(i, i + by) for i in range(count) if 0 <= i + by < count]
    return lax.ppermute(x, axis, pairs)


def lines_along_z(first):
    sizes = [lax.axis_size(axis) for axis in AXES]
    place = np.arange(math.prod(sizes)).reshape(sizes)
    lines = place.transpose(1, 2, 3, 4, 0).reshape(-1, sizes[4] * sizes[0])
    return np.roll(lines, -first, axis=1).tolist()


def along_y(x, by):
    count = lax.axis_size("y") * lax.axis_size("zhi")
    pairs = []
    for core, step in enumerate((by, -by)):
        pairs += [(core * count + i, core * count + i + step) for i in range(count) if 0 <= i + step < count]
    return lax.ppermute(x, ("core", "y", "zhi"), pairs)


def local(activations, grad_out, kernel):
    core = lax.axis_index("core")
    g = grad_out.reshape(CH, CELLS)
    a = activations.reshape(CH, CELLS)

    ahead, behind, last_face, first_face = run_rows(core, g, a)
    far = along_y(ahead, 1)
    back = along_y(behind, -1)


    weights = kernel.reshape(CH, 3, 3, ROWS).transpose(3, 2, 1, 0).reshape(ROWS, 3 * ROWS)

    below = shifted_by(last_face, "px", 1)
    above = shifted_by(first_face, "px", -1)
    inner = run_inner(g, a)
    weights, *inner = lax.optimization_barrier((weights, *inner))
    message = run_message(core, g, *inner, below, above, far)

    parts = lax.all_to_all(message, ("core", "px", "y"), 0, 0)
    mine = jnp.sum(parts, axis=0)
    mine, far = lax.optimization_barrier((mine, far))
    low = jnp.where(core == 0, far[:, :HALF], back)
    high = jnp.where(core == 0, back, far[:, :HALF])
    parts = lax.all_to_all(
        jnp.broadcast_to(mine.reshape(1, 8, 4, LANES), (4, 8, 4, LANES)).reshape(32, 4, LANES),
        AXES, 0, 0, axis_index_groups=lines_along_z(16),
    )
    last = (NX - 1) * LANES
    corner_below = shifted_by(jnp.concatenate([low[:, last:], high[:, last:]], axis=1), "px", 1)
    corner_above = shifted_by(jnp.concatenate([plane(low, 0), plane(high, 0)], axis=1), "px", -1)
    mine = jnp.sum(parts, axis=0)
    mine, g = lax.optimization_barrier((mine, g))
    grad_input = run_input(g, weights, below, above, low, high, corner_below, corner_above)
    parts = lax.all_to_all(jnp.broadcast_to(mine, (16, 4, LANES)), ("px", "y"), 0, 0)
    whole = parts.reshape(4, 16 * LANES)[:, : 9 * ROWS]
    total = 16 * 16 * 64 * 128
    return grad_input.reshape(1, CH, NX, NY, LANES), whole * (1.0 / math.sqrt(total))


def solution(mesh):
    fine = Mesh(mesh.devices.reshape(8, 2, 4, 4, 4), AXES)
    dp, py = ("zlo", "core"), ("y", "zhi")
    cells = P(dp, None, "px", py, None)
    return jax.shard_map(
        local, mesh=fine, in_specs=(cells, cells, P()), out_specs=(cells, P(dp, None)), check_vma=False
    )
```

```python
import math

import jax
import jax.numpy as jnp
import numpy as np
from jax import lax
from jax.experimental import pallas as pl
from jax.experimental.pallas import tpu as pltpu
from jax.sharding import Mesh, PartitionSpec as P

AXES = ("zlo", "core", "px", "y", "zhi")
LANES = 128
CH = 64
NX = 4
NY = 4
CELLS = NX * NY * LANES
F32 = jnp.float32
BF16 = jnp.bfloat16
ROWS = 3 * CH
HALF = NX * LANES
WIDE = (NX + 2) * LANES


def plane(ref, index):
    return ref[:, index * LANES : (index + 1) * LANES]


def shift_z(x, by):
    lane = lax.broadcasted_iota(jnp.int32, x.shape, 1)
    if by == 1:
        return jnp.where(lane == 0, 0.0, pltpu.roll(x, 1, 1))
    return jnp.where(lane == LANES - 1, 0.0, pltpu.roll(x, LANES - 1, 1))


def collect_z(t):
    return shift_z(t[0:CH], -1) + t[CH : 2 * CH] + shift_z(t[2 * CH : ROWS], 1)


def over_x(get, y):
    return [
        jnp.concatenate([get(x - (a - 1), y) for x in range(NX)], axis=1) for a in range(3)
    ]


def dot_nt(x, y):
    return lax.dot_general(x, y, (((1,), (1,)), ((), ())), preferred_element_type=F32)


def all_shifts(cells):
    cells = cells.astype(F32)
    return jnp.concatenate([shift_z(cells, 1), cells, shift_z(cells, -1)], axis=0).astype(BF16)


def inner_kernel(g_ref, a_ref, gk_ref, row_ref, column_ref, a3_ref):
    def get(x, y):
        if x < 0 or x >= NX:
            return jnp.zeros((CH, LANES), BF16)
        return plane(g_ref, x * NY + y)

    for y in range(NY):
        for x in range(NX):
            a3_ref[:, x * LANES : (x + 1) * LANES] = all_shifts(plane(a_ref, x * NY + y))
        if y in (0, NY - 1):
            at = y // (NY - 1) * HALF
            row_ref[:, at : at + HALF] = a3_ref[...]
        for side in range(2):
            at = side * HALF + y * LANES
            column_ref[:, at : at + LANES] = plane(a3_ref, side * (NX - 1))
        taps = [b for b in range(3) if 0 <= y - (b - 1) < NY]
        rows = []
        for b in taps:
            rows += over_x(get, y - (b - 1))
        first, last = (taps[0] * ROWS, (taps[-1] + 1) * ROWS)
        terms = dot_nt(jnp.concatenate(rows, axis=0), a3_ref[...])
        if y == 0:
            gk_ref[first:last, :] = terms
            gk_ref[last:, :] = jnp.zeros((3 * ROWS - last, ROWS), F32)
        else:
            gk_ref[first:last, :] += terms


def faces_kernel(
    core_ref, g_ref, gk_ref, row_ref, column_ref, below_ref, above_ref, sum_ref, rim_ref, own_ref
):
    upward = core_ref[0] == 0

    def near(low, high):
        return jnp.where(upward, low, high)

    rim_ref[:, 0:LANES] = all_shifts(near(plane(below_ref, NY), plane(below_ref, NY + 1)))
    rim_ref[:, LANES : LANES + HALF] = near(row_ref[:, 0:HALF], row_ref[:, HALF : 2 * HALF])
    rim_ref[:, LANES + HALF : WIDE] = all_shifts(near(plane(above_ref, NY), plane(above_ref, NY + 1)))
    own = [near(plane(below_ref, 0), plane(below_ref, NY - 1))]
    own += [near(plane(g_ref, x * NY), plane(g_ref, x * NY + NY - 1)) for x in range(NX)]
    own += [near(plane(above_ref, 0), plane(above_ref, NY - 1))]
    for at, cells in enumerate(own):
        own_ref[:, at * LANES : (at + 1) * LANES] = cells
    for b in range(3):
        rows = [y for y in range(NY) if 0 <= y - (b - 1) < NY]
        of_g = (rows[0] - (b - 1)) * LANES
        size = len(rows) * LANES
        for a, face, side in ((0, above_ref, 1), (1, None, 0), (2, below_ref, 0)):
            at = b * ROWS + a * CH
            value = gk_ref[at : at + CH, :]
            if face is not None:
                of_a = side * HALF + rows[0] * LANES
                value += dot_nt(face[:, of_g : of_g + size], column_ref[:, of_a : of_a + size])
            sum_ref[at : at + CH, :] = value


def message_kernel(core_ref, gk_ref, rim_ref, own_ref, far_ref, msg_ref, wide_ref, far3_ref):
    upward = core_ref[0] == 0
    for x in range(NX):
        far3_ref[:, x * LANES : (x + 1) * LANES] = all_shifts(plane(far_ref, NX + x))

    def across(a):
        at = (2 - a) * LANES
        of_far = dot_nt(far_ref[:, 0:HALF], rim_ref[:, a * LANES : a * LANES + HALF])
        of_own = dot_nt(own_ref[:, at : at + HALF], far3_ref[...])
        return jnp.where(upward, of_own, of_far), jnp.where(upward, of_far, of_own)

    pairs = [across(a) for a in range(3)]

    def block(a, b):
        value = gk_ref[b * ROWS + a * CH : b * ROWS + (a + 1) * CH, :]
        return value if b == 1 else value + pairs[a][b // 2]

    pad = jnp.zeros((CH, 2 * LANES - ROWS), F32)
    lane = lax.broadcasted_iota(jnp.int32, (CH, LANES), 1)
    for m in range(5):
        even = jnp.concatenate([block(*divmod(2 * m, 3)), pad], axis=1)
        wide_ref[3 * m] = even[:, 0:LANES]
        if m == 4:
            wide_ref[3 * m + 1] = even[:, LANES:]
            wide_ref[3 * m + 2] = jnp.zeros((CH, LANES), F32)
            wide_ref[3 * m + 3] = jnp.zeros((CH, LANES), F32)
            break
        odd = jnp.concatenate([block(*divmod(2 * m + 1, 3)), pad], axis=1)
        odd = pltpu.roll(odd, CH, 1)
        wide_ref[3 * m + 1] = jnp.where(lane < CH, even[:, LANES:], odd[:, 0:LANES])
        wide_ref[3 * m + 2] = odd[:, LANES:]
    for s in range(8):
        for column in range(16):
            at = column % 4 * LANES
            msg_ref[s * 4 + column // 4, :, at : at + LANES] = wide_ref[
                column, pl.ds(s, 8, stride=8), :
            ]


def input_kernel(
    g_ref, w_ref, below_ref, above_ref, low_ref, high_ref, corner_below_ref, corner_above_ref, out_ref
):
    def get(x, y):
        if 0 <= y < NY:
            if x < 0:
                return plane(below_ref, y)
            if x >= NX:
                return plane(above_ref, y)
            return plane(g_ref, x * NY + y)
        side = 0 if y < 0 else 1
        if x < 0:
            return plane(corner_below_ref, side)
        if x >= NX:
            return plane(corner_above_ref, side)
        return plane((low_ref, high_ref)[side], x)

    for y in range(NY):
        rows = []
        for b in range(3):
            rows += over_x(get, y - (b - 1))
        t = jnp.dot(w_ref[...], jnp.concatenate(rows, axis=0), preferred_element_type=F32)
        for x in range(NX):
            lanes = (x * NY + y) * LANES
            out_ref[:, lanes : lanes + LANES] = collect_z(
                t[:, x * LANES : (x + 1) * LANES]
            ).astype(BF16)


def call(body, out_shape, scratch=(), cost=None, **specs):
    return pl.pallas_call(
        body,
        out_shape=out_shape,
        scratch_shapes=scratch,
        cost_estimate=cost,
        compiler_params=pltpu.CompilerParams(vmem_limit_bytes=48 * 1024 * 1024),
        **specs,
    )


def run_inner(*operands):
    shape = jax.ShapeDtypeStruct
    return call(
        inner_kernel,
        (shape((3 * ROWS, ROWS), F32), shape((ROWS, 2 * HALF), BF16), shape((ROWS, 2 * HALF), BF16)),
        [pltpu.VMEM((ROWS, HALF), BF16)],
    )(*operands)


def with_core(body, out_shape, scratch, core, operands):
    vmem = pl.BlockSpec(memory_space=pltpu.VMEM)
    return call(
        body,
        out_shape,
        scratch,
        in_specs=[pl.BlockSpec(memory_space=pltpu.SMEM)] + [vmem] * len(operands),
        out_specs=jax.tree.map(lambda _: vmem, out_shape),
    )(core.reshape(1), *operands)


def run_faces(core, *operands):
    shape = jax.ShapeDtypeStruct
    out_shape = (shape((3 * ROWS, ROWS), F32), shape((ROWS, WIDE), BF16), shape((CH, WIDE), BF16))
    return with_core(faces_kernel, out_shape, (), core, operands)


def run_message(core, *operands):
    out_shape = jax.ShapeDtypeStruct((32, 8, HALF), F32)
    scratch = [pltpu.VMEM((16, CH, LANES), F32), pltpu.VMEM((ROWS, HALF), BF16)]
    return with_core(message_kernel, out_shape, scratch, core, operands)


def rows_kernel(core_ref, g_ref, a_ref, ahead_ref, behind_ref, last_ref, first_ref):
    upward = core_ref[0] == 0
    for x in range(NX):
        low, high = (x * NY, x * NY + NY - 1)
        lanes = slice(x * LANES, (x + 1) * LANES)
        ahead_ref[:, lanes] = jnp.where(upward, plane(g_ref, high), plane(g_ref, low))
        behind_ref[:, lanes] = jnp.where(upward, plane(g_ref, low), plane(g_ref, high))
        lanes = slice(HALF + x * LANES, HALF + (x + 1) * LANES)
        ahead_ref[:, lanes] = jnp.where(upward, plane(a_ref, high), plane(a_ref, low))
    size = NY * LANES
    for x, out_ref in ((NX - 1, last_ref), (0, first_ref)):
        out_ref[:, 0:size] = g_ref[:, x * size : (x + 1) * size]
        out_ref[:, size : size + LANES] = plane(a_ref, x * NY)
        out_ref[:, size + LANES : size + 2 * LANES] = plane(a_ref, x * NY + NY - 1)


def run_rows(core, *operands):
    vmem = pl.BlockSpec(memory_space=pltpu.VMEM)
    return call(
        rows_kernel,
        tuple(jax.ShapeDtypeStruct((CH, n * LANES), BF16) for n in (2 * NX, NX, 6, 6)),
        in_specs=[pl.BlockSpec(memory_space=pltpu.SMEM), vmem, vmem],
        out_specs=(vmem,) * 4,
    )(core.reshape(1), *operands)


def run_input(*operands):
    return call(input_kernel, jax.ShapeDtypeStruct((CH, CELLS), BF16))(*operands)


def shifted_by(x, axis, by):
    count = lax.axis_size(axis)
    pairs = [(i, i + by) for i in range(count) if 0 <= i + by < count]
    return lax.ppermute(x, axis, pairs)


def lines_along_z(first):
    sizes = [lax.axis_size(axis) for axis in AXES]
    place = np.arange(math.prod(sizes)).reshape(sizes)
    lines = place.transpose(1, 2, 3, 4, 0).reshape(-1, sizes[4] * sizes[0])
    return np.roll(lines, -first, axis=1).tolist()


def along_y(x, by):
    count = lax.axis_size("y") * lax.axis_size("zhi")
    pairs = []
    for core, step in enumerate((by, -by)):
        pairs += [(core * count + i, core * count + i + step) for i in range(count) if 0 <= i + step < count]
    return lax.ppermute(x, ("core", "y", "zhi"), pairs)


def local(activations, grad_out, kernel):
    core = lax.axis_index("core")
    g = grad_out.reshape(CH, CELLS)
    a = activations.reshape(CH, CELLS)

    ahead, behind, last_face, first_face = run_rows(core, g, a)
    far = along_y(ahead, 1)
    back = along_y(behind, -1)


    weights = kernel.reshape(CH, 3, 3, ROWS).transpose(3, 2, 1, 0).reshape(ROWS, 3 * ROWS)

    below = shifted_by(last_face, "px", 1)
    above = shifted_by(first_face, "px", -1)
    inner = run_inner(g, a)
    weights, *inner = lax.optimization_barrier((weights, *inner))
    message = run_message(core, *run_faces(core, g, *inner, below, above), far)

    parts = lax.all_to_all(message, ("core", "px", "y"), 0, 0)
    mine = jnp.sum(parts, axis=0)
    mine, far = lax.optimization_barrier((mine, far))
    low = jnp.where(core == 0, far[:, :HALF], back)
    high = jnp.where(core == 0, back, far[:, :HALF])
    parts = lax.all_to_all(
        jnp.broadcast_to(mine.reshape(1, 8, 4, LANES), (4, 8, 4, LANES)).reshape(32, 4, LANES),
        AXES, 0, 0, axis_index_groups=lines_along_z(16),
    )
    last = (NX - 1) * LANES
    corner_below = shifted_by(jnp.concatenate([low[:, last:], high[:, last:]], axis=1), "px", 1)
    corner_above = shifted_by(jnp.concatenate([plane(low, 0), plane(high, 0)], axis=1), "px", -1)
    mine = jnp.sum(parts, axis=0)
    mine, g = lax.optimization_barrier((mine, g))
    grad_input = run_input(g, weights, below, above, low, high, corner_below, corner_above)
    parts = lax.all_to_all(jnp.broadcast_to(mine, (16, 4, LANES)), ("px", "y"), 0, 0)
    whole = parts.reshape(4, 16 * LANES)[:, : 9 * ROWS]
    total = 16 * 16 * 64 * 128
    return grad_input.reshape(1, CH, NX, NY, LANES), whole * (1.0 / math.sqrt(total))


def solution(mesh):
    fine = Mesh(mesh.devices.reshape(8, 2, 4, 4, 4), AXES)
    dp, py = ("zlo", "core"), ("y", "zhi")
    cells = P(dp, None, "px", py, None)
    return jax.shard_map(
        local, mesh=fine, in_specs=(cells, cells, P()), out_specs=(cells, P(dp, None)), check_vma=False
    )
```
